128 devices in a mesh: gx: 16 (over z, y_hi, core), gy: 8 (over y_lo, x).
Axes of the slice: x: 4, y: 4 (y_hi: 2, y_lo: 2; y = y_hi * 2 + y_lo), z: 4, core: 2. Of those that a mesh axis runs over, the one named last changes fastest.
Arguments:
- temp_fluid: float32 [256, 512, 1024], P('gx', 'gy'), may hold values from -6 to 6
- velocity: bfloat16 [3, 256, 512, 1024], P(None, 'gx', 'gy'), may hold values from -1 to 1
- wall_old: float32 [256, 512, 128], P('gx', 'gy'), may hold values from -6 to 6
- wall_mask: int32 [256, 512, 128], P('gx', 'gy'), may hold values 0 or 1
- owner_map: int32 [128, 1024, 1], P(('gx', 'gy')), may hold values from 0 to 127; in each aligned block of 1024 rows (0 to 1023, 1024 to 2047, ..., all dimensions but the last counted through in order) at most 24 rows name the same one
- slot_map: int32 [128, 1024], P(('gx', 'gy')), may hold values from 0 to 511
- temp_solid: float32 [256, 256, 128], P('gx', 'gy'), may hold values from -6 to 6
- material: int32 [256, 256, 128], P('gx', 'gy'), may hold values from 0 to 3
Outputs:
- fluid_next: float32 [256, 512, 1024], P('gx', 'gy')
- wall_next: float32 [256, 512, 128], P('gx', 'gy')
- solid_next: float32 [256, 256, 128], P('gx', 'gy')
- stress_force: float32 [3, 256, 256, 128], P(None, 'gx', 'gy')
The draws below stay inside these ranges and needn't reach their ends.
Inputs may be any that keep to these rules, and one draw needn't show every extreme that they name: `owner_map`: among the rows of one device, no owner is named by more than 24 rows, a bound that some block reaches.
All inputs are finite; a program needn't handle non-finite values. No bound on the sum of `wall_mask` on one device may be relied on, other than what follows from the above.
Results may differ from the reference program's by a relative error of at most 0.0003.
Values sent between devices are 32-bit elements; how exact they have to be, the bound alone decides.
A program may use at most 128 MiB of HBM per device.

```python
import math
import jax
import jax.numpy as jnp
import numpy as np

CX = 16
CY = 64
NZ = 1024
ROW = 128
SX = 16
SY = 32
FSTEPS = 2
SSTEPS = 4
NMAT = 4
SZ = 128
NX = 256
NY = 512
SXG = 256
SYG = 256
ROWS = 1024
SLOTS = 512
CAP = 24
N_GX = 16
N_GY = 8
DEVICES = 128


def place_ends(array, own_key, low, largest):
    longest = array.shape.index(max(array.shape))
    spots = []
    for shift in (0, 1):
        where = [jax.random.randint(jax.random.fold_in(own_key, axis), (), 0, length) for axis, length in enumerate(array.shape)]
        where[longest] = (where[longest] + shift) % array.shape[longest]
        spots.append(tuple(where))
    return array.at[spots[0]].set(low).at[spots[1]].set(largest)


def level_of(stream_key, dims, pieces, smallest, top_value):
    loudness, own = 1.0, jax.random.fold_in(stream_key, 6)
    for position, parts in pieces:
        heights = jnp.exp(jax.random.uniform(jax.random.fold_in(own, position), (parts,), jnp.float32, smallest / len(pieces), top_value / len(pieces)))
        loudness = loudness * jnp.repeat(heights, dims[position] // parts).reshape([-1 if axis == position else 1 for axis in range(len(dims))])
    return loudness


def deal_out(own_key, own, number, rows, amount, top, most, skew):
    order = jax.random.permutation(own_key, amount)
    packed, ordinary = load_shares(amount, rows * top, most, skew, True), load_shares(amount, rows * top, most, skew, False)
    places = jnp.arange(amount)

    def named(sizes, turn):
        used = int((sizes > 0).sum())
        fixed = max(1, used // 4)
        shifted = fixed + (places - fixed + turn * (used - fixed)) % max(1, amount - fixed)
        return jnp.zeros((amount,), jnp.int32).at[order[jnp.where(places < fixed, places, shifted)]].set(jnp.asarray(sizes, jnp.int32))

    sizes = jnp.where(number % 4 == 0, named(packed, number // 4), named(ordinary, number - number // 4 - 1))
    mixed = jax.random.permutation(jax.random.fold_in(own, 3), amount)
    source_of, receiver = mixed[0:amount // 2 * 2:2], mixed[1:amount // 2 * 2:2]
    margin = jnp.minimum(sizes[source_of] - 1, most - sizes[receiver]) // 2
    margin = jnp.where((source_of == order[0]) | (receiver == order[0]) | (sizes[receiver] == 0), 0, jnp.maximum(margin, 0))
    shifted = jax.random.randint(jax.random.fold_in(own, 4), (amount // 2,), 0, 1 << 20) % (margin + 1)
    sizes = sizes.at[source_of].add(-shifted).at[receiver].add(shifted)
    labels = jnp.searchsorted(jnp.cumsum(sizes), jnp.arange(rows * top), side="right").astype(jnp.int32)
    listing = labels.reshape(top, rows).T
    listing = listing[jax.random.permutation(jax.random.fold_in(own, 1), rows)]
    turn = jax.random.randint(jax.random.fold_in(own, 2), (rows, 1), 0, top)
    return jnp.take_along_axis(listing, (jnp.arange(top)[None, :] + turn) % top, axis=1)


def load_shares(number_of, total, limit, lean, full):
    weights = [(1 << 20) // math.isqrt(standing ** lean) + 1 for standing in range(1, number_of + 1)]
    largest = limit if full else min(limit, max(-(-total // number_of), total * weights[0] // sum(weights)))
    least = 1 if total - largest >= number_of - 1 else 0
    holding, surplus = [largest] + [least] * (number_of - 1), total - largest - least * (number_of - 1)
    while surplus > 0:
        free = [i for i in range(1, number_of) if holding[i] < largest] or [i for i in range(1, number_of) if holding[i] < limit]
        mass, left = sum([weights[i] for i in free]), surplus
        for i in free:
            extra = min(limit - holding[i], max(1, left * weights[i] // mass), surplus)
            holding[i] = holding[i] + extra
            surplus = surplus - extra
    return np.array(holding)


def centred(stream_key, extent, width, most, cuts=(), dtype=jnp.bfloat16):
    entries = jax.random.normal(stream_key, extent, jnp.float32) * width
    if len(cuts) > 0:
        entries = level_of(stream_key, extent, cuts, -0.22, 0.18) * entries
    return jnp.clip(entries, min=-most, max=most).astype(dtype)


def setup_inputs(seed: int = 0) -> dict:
    keys = jax.random.split(jax.random.key(seed), 9)
    temp_fluid = centred(keys[0], (NX, NY, NZ), 1.0, 6.0, ((0, 16), (1, 8)), jnp.float32)
    velocity = jnp.clip(jax.random.uniform(keys[1], (3, NX, NY, NZ), jnp.float32, -1.0, 1.0) * level_of(keys[1], (3, NX, NY, NZ), ((1, 16), (2, 8)), -0.4, 0.0), -1.0, 1.0).astype(jnp.bfloat16)
    wall_old = centred(keys[2], (NX, NY, ROW), 1.0, 6.0, ((0, 16), (1, 8)), jnp.float32)
    wall_mask = place_ends((jax.random.randint(keys[3], (NX, NY, ROW), 0, 4) < 3).astype(jnp.int32), jax.random.fold_in(keys[3], 1), 0, 1)
    owner_map_keys = jax.random.split(jax.random.fold_in(keys[4], 1), DEVICES * ROWS // ROWS)
    owner_map_turns = jax.random.permutation(jax.random.fold_in(keys[4], 3), DEVICES * ROWS // ROWS)
    owner_map = jax.vmap(lambda own, number: deal_out(jax.random.fold_in(keys[4], 2), own, number, ROWS, DEVICES, 1, CAP, 2))(owner_map_keys, owner_map_turns).reshape((DEVICES, ROWS, 1))
    slot_map = place_ends(jax.random.randint(keys[5], (DEVICES, ROWS), 0, SLOTS), jax.random.fold_in(keys[5], 1), 0, SLOTS - 1).astype(jnp.int32)
    temp_solid = centred(keys[6], (SXG, SYG, SZ), 1.0, 6.0, ((0, 16), (1, 8)), jnp.float32)
    material = place_ends(jax.random.randint(keys[7], (SXG, SYG, SZ), 0, NMAT), jax.random.fold_in(keys[7], 1), 0, NMAT - 1).astype(jnp.int32)
    return dict(temp_fluid=temp_fluid, velocity=velocity, wall_old=wall_old, wall_mask=wall_mask, owner_map=owner_map, slot_map=slot_map, temp_solid=temp_solid, material=material)


time_step = 0.1
diffusivity = 0.5
film_coef = 2.0
solid_step = 0.05
source_gain = 4.0
conduct_table = (0.4, 0.9, 1.5, 2.2)
modulus_table = (0.5, 1.0, 1.6, 2.4)


def laplace(padded):
    center = padded[1:-1, 1:-1, 1:-1]
    beside = padded[2:, 1:-1, 1:-1] + padded[:-2, 1:-1, 1:-1]
    beside = beside + padded[1:-1, 2:, 1:-1] + padded[1:-1, :-2, 1:-1]
    beside = beside + padded[1:-1, 1:-1, 2:] + padded[1:-1, 1:-1, :-2]
    return beside - 6.0 * center


def advect(padded, velocity):
    center = padded[1:-1, 1:-1, 1:-1]
    uppers = (padded[2:, 1:-1, 1:-1], padded[1:-1, 2:, 1:-1], padded[1:-1, 1:-1, 2:])
    lowers = (padded[:-2, 1:-1, 1:-1], padded[1:-1, :-2, 1:-1], padded[1:-1, 1:-1, :-2])
    total = jnp.zeros_like(center)
    for comp in range(3):
        speed = velocity[comp].astype(jnp.float32)
        total = total + jnp.maximum(speed, 0.0) * (center - lowers[comp]) + jnp.minimum(speed, 0.0) * (uppers[comp] - center)
    return total


def fluid_update(padded, velocity, sink):
    center = padded[1:-1, 1:-1, 1:-1]
    return center + time_step * (diffusivity * laplace(padded) - advect(padded, velocity)) - time_step * sink


def table_lookup(material, table):
    out = jnp.zeros(material.shape, jnp.float32)
    for index in range(NMAT):
        out = out + jnp.where(material == index, table[index], 0.0).astype(jnp.float32)
    return out


def solid_update(padded, cond, heat):
    center = padded[1:-1, 1:-1, 1:-1]
    return center + solid_step * (cond * laplace(padded) + source_gain * heat)


def gradient(padded):
    first = 0.5 * (padded[2:, 1:-1, 1:-1] - padded[:-2, 1:-1, 1:-1])
    second = 0.5 * (padded[1:-1, 2:, 1:-1] - padded[1:-1, :-2, 1:-1])
    third = 0.5 * (padded[1:-1, 1:-1, 2:] - padded[1:-1, 1:-1, :-2])
    return jnp.stack([first, second, third])


def reference(temp_fluid, velocity, wall_old, wall_mask, owner_map, slot_map, temp_solid, material):
    flux = wall_mask.astype(jnp.float32) * film_coef * (temp_fluid[:, :, :ROW] - wall_old)
    flux_rows = flux.reshape(N_GX, CX, N_GY, CY, ROW).transpose(0, 2, 1, 3, 4).reshape(DEVICES, ROWS, ROW)
    owner = owner_map[:, :, 0]
    solid_x = (owner // N_GY) * SX + slot_map // SY
    solid_y = (owner % N_GY) * SY + slot_map % SY
    heat = jnp.zeros((SXG, SYG, SZ), jnp.float32).at[solid_x, solid_y].add(flux_rows)
    sink = jnp.concatenate([flux, jnp.zeros((NX, NY, NZ - ROW), jnp.float32)], axis=2)
    fluid = temp_fluid
    for step in range(FSTEPS):
        fluid = fluid_update(jnp.pad(fluid, 1), velocity, sink)
    cond = table_lookup(material, conduct_table)
    modulus = table_lookup(material, modulus_table)
    solid = temp_solid
    for step in range(SSTEPS):
        solid = solid_update(jnp.pad(solid, 1), cond, heat)
    stress_force = gradient(jnp.pad(modulus * solid, 1))
    returned = solid[solid_x, solid_y]
    wall_next = returned.reshape(N_GX, N_GY, CX, CY, ROW).transpose(0, 2, 1, 3, 4).reshape(NX, NY, ROW)
    return fluid, wall_next, solid, stress_force
```

```python
import functools

import jax
import jax.numpy as jnp
from jax import lax
from jax.experimental import pallas as pl
from jax.experimental.pallas import tpu as pltpu
from jax.sharding import PartitionSpec as P

MESH = pl.DeviceIdType.MESH
F32 = jnp.float32
BF16 = jnp.bfloat16
I32 = jnp.int32

NGX, NGY = 16, 8
NDEV = 128
CX, CY, NT, LN = 16, 64, 8, 128
SX, SY = 16, 32
CAP = 24
ROWS = 1024
SLOTS = 512
PADY = 8
WT = 5
WH = 4
SP = SX + 2 * WT
SR = 64
R0 = 16
CONDUCT = (0.4, 0.9, 1.5, 2.2)
MODULUS = (0.5, 1.0, 1.6, 2.4)
DIRS = [(dx, dy) for dx in (-1, 0, 1) for dy in (-1, 0, 1) if (dx, dy) != (0, 0)]


def peer_of(gx, gy, k):
    dc, dx, dy, dz = k & 1, (k >> 1) & 3, (k >> 3) & 3, (k >> 5) & 3
    c, z, x, y = gx & 1, gx >> 2, gy & 3, (gx & 2) | (gy >> 2)
    nc, nx, ny, nz = c ^ dc, (x + dx) & 3, (y + dy) & 3, (z + dz) & 3
    return (nz << 2) | (ny & 2) | nc, ((ny & 1) << 2) | nx


def halves(value):
    hi = value.astype(BF16)
    lo = (value - hi.astype(F32)).astype(BF16)
    return jnp.concatenate([hi, lo], axis=1)


def joined(product):
    return product[:, :LN] + product[:, LN:]


def onehot(mask):
    return jnp.where(mask, 1.0, 0.0).astype(BF16)


def lookup(material, table):
    out = jnp.where(material == 0, table[0], 0.0)
    for index in range(1, 4):
        out = jnp.where(material == index, table[index], out)
    return out.astype(F32)


def planes(step, width):
    if step > 0:
        return pl.ds(WT + SX - width, width), pl.ds(WT - width, width)
    if step < 0:
        return pl.ds(WT, width), pl.ds(WT + SX, width)
    return pl.ds(WT, SX), pl.ds(WT, SX)


def lines(step):
    if step > 0:
        return pl.ds(R0 + SY - 8, 8), pl.ds(R0 - 8, 8)
    if step < 0:
        return pl.ds(R0, 8), pl.ds(R0 + SY, 8)
    return pl.ds(R0, SY), pl.ds(R0, SY)


def inside(gx, gy, dx, dy):
    px, py = gx + dx, gy + dy
    return (px >= 0) & (px < NGX) & (py >= 0) & (py < NGY)


def spread_copies(ref, gx, gy, width, sends, recvs):
    out = []
    for i, (dx, dy) in enumerate(DIRS):
        xs, xd = planes(dx, width)
        ys, yd = lines(dy)
        copy = pltpu.make_async_remote_copy(
            src_ref=ref.at[xs, ys, :],
            dst_ref=ref.at[xd, yd, :],
            send_sem=sends.at[i],
            recv_sem=recvs.at[i],
            device_id=(gx + dx, gy + dy),
            device_id_type=MESH,
        )
        out.append((copy, inside(gx, gy, dx, dy), inside(gx, gy, -dx, -dy)))
    return out


def start_all(copies):
    for copy, to, _ in copies:
        pl.when(to)(copy.start)


def wait_recvs(copies):
    for copy, _, came in copies:
        pl.when(came)(copy.wait_recv)


def wait_sends(copies):
    for copy, to, _ in copies:
        pl.when(to)(copy.wait_send)


def face_copies(field, ysend, yrecv, gx, gy, sends, recvs):
    out = []
    rows = pl.ds(PADY, CY)
    for i, step in enumerate((1, -1)):
        src, dst = (CX, 0) if step > 0 else (1, CX + 1)
        copy = pltpu.make_async_remote_copy(
            src_ref=field.at[:, src, rows, :],
            dst_ref=field.at[:, dst, rows, :],
            send_sem=sends.at[i],
            recv_sem=recvs.at[i],
            device_id=(gx + step, gy),
            device_id_type=MESH,
        )
        out.append((copy, inside(gx, gy, step, 0), inside(gx, gy, -step, 0)))
    for i, step in enumerate((1, -1)):
        copy = pltpu.make_async_remote_copy(
            src_ref=ysend.at[i],
            dst_ref=yrecv.at[i],
            send_sem=sends.at[2 + i],
            recv_sem=recvs.at[2 + i],
            device_id=(gx, gy + step),
            device_id_type=MESH,
        )
        out.append((copy, inside(gx, gy, 0, step), inside(gx, gy, 0, -step)))
    return out


def take_faces(field, ysend):
    for t in range(NT):
        ysend[0, t] = field[t, 1 : CX + 1, PADY + CY - 1, :]
        ysend[1, t] = field[t, 1 : CX + 1, PADY, :]


def put_faces(field, yrecv):
    for t in range(NT):
        field[t, 1 : CX + 1, PADY - 1, :] = yrecv[0, t]
        field[t, 1 : CX + 1, PADY + CY, :] = yrecv[1, t]


def fluid_plane(src, dst, vel, flux, x):
    lane = lax.broadcasted_iota(I32, (16, LN), 1)
    first, last = lane == 0, lane == LN - 1
    zero = jnp.zeros((16, LN), F32)
    for h in range(CY // 16):
        r = PADY + 16 * h
        mids = [src[t, x + 1, r : r + 16, :] for t in range(NT)]
        ups = [pltpu.roll(c, LN - 1, 1) for c in mids] + [zero]
        downs = [zero] + [pltpu.roll(c, 1, 1) for c in mids]
        for t in range(NT):
            c = mids[t]
            pairs = (
                (src[t, x + 2, r : r + 16, :], src[t, x, r : r + 16, :]),
                (src[t, x + 1, r + 1 : r + 17, :], src[t, x + 1, r - 1 : r + 15, :]),
                (jnp.where(last, ups[t + 1], ups[t]), jnp.where(first, downs[t], downs[t + 1])),
            )
            total = None
            for k, (p, m) in enumerate(pairs):
                u = vel[k, x, 16 * h : 16 * h + 16, t * LN : (t + 1) * LN].astype(F32)
                a = jnp.maximum(u + 0.5, 0.5)
                pc = p - c
                term = a * ((m - c) + pc) - u * pc
                total = term if total is None else total + term
            if t == 0:
                total = total - flux[pl.ds(pl.multiple_of(x * CY + 16 * h, 16), 16), :]
            dst[t, x + 1, r : r + 16, :] = c + 0.1 * total


def solid_step(src, dst, cond, heat, low, high):
    lane = lax.broadcasted_iota(I32, (SR - 16, LN), 1)

    def one(x, carry):
        c = src[x, 8 : SR - 8, :]
        zp = jnp.where(lane == LN - 1, 0.0, pltpu.roll(c, LN - 1, 1))
        zm = jnp.where(lane == 0, 0.0, pltpu.roll(c, 1, 1))
        beside = src[x + 1, 8 : SR - 8, :] + src[x - 1, 8 : SR - 8, :]
        beside = beside + src[x, 9 : SR - 7, :] + src[x, 7 : SR - 9, :]
        beside = beside + zp + zm
        lap = beside - 6.0 * c
        dst[x, 8 : SR - 8, :] = c + 0.05 * (
            cond[x, 8 : SR - 8, :] * lap + 4.0 * heat[x, 8 : SR - 8, :]
        )
        return carry

    lax.fori_loop(low, high, one, 0)


def kernel(
    fluid_in, vel_in, wall_in, mask_in, owner_in, slot_in, solid_in, mat_in,
    fluid_out, wall_out, solid_out, stress_out,
    f0, f1, vel, wall, mask, flux, owner, slot, dest, dest_s,
    outgoing, incoming, replies, returned, meta_out, meta_in,
    s0, s1, mat, cond, heat, ysend, yrecv,
    in_sem, out_sem, self_sem, a2a_sem, fsend, frecv, ssend, srecv,
):
    gx, gy = lax.axis_index("gx"), lax.axis_index("gy")
    me = gx * NGY + gy

    loads = [
        pltpu.make_async_copy(owner_in, owner, in_sem.at[0]),
        pltpu.make_async_copy(slot_in, slot, in_sem.at[1]),
        pltpu.make_async_copy(wall_in, wall, in_sem.at[2]),
        pltpu.make_async_copy(mask_in, mask, in_sem.at[3]),
    ]
    interior = (pl.ds(1, CX), pl.ds(PADY, CY))
    tiles = [
        pltpu.make_async_copy(
            fluid_in.at[:, :, pl.ds(t * LN, LN)], f0.at[t, interior[0], interior[1], :], in_sem.at[4 + t]
        )
        for t in range(NT)
    ]
    core = (pl.ds(WT, SX), pl.ds(R0, SY))
    load_solid = pltpu.make_async_copy(solid_in, s0.at[core[0], core[1], :], in_sem.at[12])
    load_mat = pltpu.make_async_copy(mat_in, mat.at[core[0], core[1], :], in_sem.at[13])
    load_vel = pltpu.make_async_copy(vel_in, vel, in_sem.at[14])

    for ld in loads[:2]:
        ld.start()
    tiles[0].start()
    for ld in loads[2:]:
        ld.start()

    for field in (f0, f1):
        for t in range(NT):
            for x in (0, CX + 1):
                field[t, x] = jnp.zeros((CY + 2 * PADY, LN), F32)
    yrecv[...] = jnp.zeros_like(yrecv)

    def clear(x, carry):
        for ref, value in ((s0, 0.0), (heat, 0.0), (mat, -1)):
            ref[x, 8:R0, :] = jnp.full((8, LN), value, ref.dtype)
            ref[x, R0 + SY : R0 + SY + 8, :] = jnp.full((8, LN), value, ref.dtype)
        return carry

    lax.fori_loop(0, SP, clear, 0)
    for x in list(range(WT)) + list(range(WT + SX, SP)):
        for ref, value in ((s0, 0.0), (heat, 0.0), (mat, -1)):
            ref[x, R0 : R0 + SY, :] = jnp.full((SY, LN), value, ref.dtype)

    barrier = pltpu.get_barrier_semaphore()

    def greet(k, carry):
        px, py = peer_of(gx, gy, (k * 37) & 127)
        pl.semaphore_signal(barrier, inc=1, device_id=(px, py), device_id_type=MESH)
        return carry

    lax.fori_loop(1, NDEV, greet, 0)
    load_solid.start()
    load_mat.start()
    for t in range(1, NT):
        tiles[t].start()
    load_vel.start()

    loads[0].wait()
    loads[1].wait()
    own_row = owner[...]
    mine = own_row == lax.broadcasted_iota(I32, (NDEV, ROWS), 0)
    mine_b = onehot(mine)
    before = onehot(
        lax.broadcasted_iota(I32, (ROWS, ROWS), 0) < lax.broadcasted_iota(I32, (ROWS, ROWS), 1)
    )
    ranks = jnp.dot(mine_b, before, preferred_element_type=F32)
    rank_row = jnp.sum(jnp.where(mine, ranks, 0.0), axis=0, keepdims=True).astype(I32)
    dest[...] = jnp.clip(own_row * CAP + rank_row, 0, NDEV * CAP - 1)
    place = pltpu.make_async_copy(dest, dest_s, in_sem.at[15])
    place.start()
    code = slot[...] + 1
    at_rank = onehot(rank_row == lax.broadcasted_iota(I32, (LN, ROWS), 0))
    parts = []
    for part in (code & 15, code >> 4):
        left = jnp.where(mine, part.astype(F32), 0.0).astype(BF16)
        parts.append(
            lax.dot_general(left, at_rank, (((1,), (1,)), ((), ())), preferred_element_type=F32)
        )
    meta_out[...] = (parts[0] + 16.0 * parts[1]).reshape(NDEV, 1, LN)

    for ld in loads[2:]:
        ld.wait()
    tiles[0].wait()
    for x in range(CX):
        t0 = f0[0, x + 1, PADY : PADY + CY, :]
        flux[x * CY : (x + 1) * CY, :] = mask[x].astype(F32) * 2.0 * (t0 - wall[x])
    flux_b = halves(flux[...])
    chunk = 16 * CAP

    def pack(i, carry):
        base = pl.multiple_of(i * chunk, chunk)
        pick = onehot(dest[...] == lax.broadcasted_iota(I32, (chunk, ROWS), 0) + base)
        outgoing[pl.ds(base, chunk), :] = joined(jnp.dot(pick, flux_b, preferred_element_type=F32))
        return carry

    lax.fori_loop(0, NDEV // 16, pack, 0)

    pl.semaphore_wait(barrier, NDEV - 1)

    def block(ref, d):
        return ref.at[pl.ds(pl.multiple_of(d * CAP, CAP), CAP), :]

    def send_rows(k, carry):
        px, py = peer_of(gx, gy, (k * 37) & 127)
        other = px * NGY + py
        pltpu.make_async_remote_copy(
            meta_out.at[other], meta_in.at[me], a2a_sem.at[0], a2a_sem.at[1],
            device_id=(px, py), device_id_type=MESH,
        ).start()
        pltpu.make_async_remote_copy(
            block(outgoing, other), block(incoming, me), a2a_sem.at[2], a2a_sem.at[3],
            device_id=(px, py), device_id_type=MESH,
        ).start()
        return carry

    lax.fori_loop(1, NDEV, send_rows, 0)
    own_meta = pltpu.make_async_copy(meta_out.at[me], meta_in.at[me], self_sem.at[0])
    own_rows = pltpu.make_async_copy(block(outgoing, me), block(incoming, me), self_sem.at[1])
    own_meta.start()
    own_rows.start()

    load_solid.wait()
    load_mat.wait()
    temp_copies = spread_copies(s0, gx, gy, WT, ssend.at[0], srecv.at[0])
    mat_copies = spread_copies(mat, gx, gy, WT, ssend.at[1], srecv.at[1])
    start_all(temp_copies)
    start_all(mat_copies)

    for t in range(1, NT):
        tiles[t].wait()
    take_faces(f0, ysend.at[0])
    faces0 = face_copies(f0, ysend.at[0], yrecv.at[0], gx, gy, fsend.at[0], frecv.at[0])
    start_all(faces0)
    load_vel.wait()
    wait_recvs(faces0)
    put_faces(f0, yrecv.at[0])

    def step_one(x, carry):
        fluid_plane(f0, f1, vel, flux, x)
        return carry

    lax.fori_loop(0, CX, step_one, 0)

    take_faces(f1, ysend.at[1])
    faces1 = face_copies(f1, ysend.at[1], yrecv.at[1], gx, gy, fsend.at[1], frecv.at[1])
    start_all(faces1)

    wait_recvs(temp_copies)
    wait_recvs(mat_copies)

    def conduct(x, carry):
        cond[x, 8 : SR - 8, :] = lookup(mat[x, 8 : SR - 8, :], CONDUCT)
        return carry

    lax.fori_loop(0, SP, conduct, 0)

    count = (NDEV - 1) * CAP
    own_meta.wait()
    own_rows.wait()
    pltpu.make_async_copy(meta_in.at[pl.ds(0, NDEV - 1)], meta_in.at[pl.ds(0, NDEV - 1)], a2a_sem.at[1]).wait()
    pltpu.make_async_copy(incoming.at[pl.ds(0, count)], incoming.at[pl.ds(0, count)], a2a_sem.at[3]).wait()
    slots_in = meta_in[...].reshape(NDEV, LN)
    slots_t = slots_in.T
    wanted = lax.broadcasted_iota(I32, (SLOTS, NDEV), 0).astype(F32) + 1.0
    total = jnp.zeros((SLOTS, 2 * LN), F32)
    for k in range(CAP):
        hit = onehot(slots_t[k : k + 1, :] == wanted)
        rows = halves(incoming[pl.ds(k, NDEV, stride=CAP), :])
        total = total + jnp.dot(hit, rows, preferred_element_type=F32)
    heat[WT : WT + SX, R0 : R0 + SY, :] = joined(total).reshape(SX, SY, LN)
    heat_copies = spread_copies(heat, gx, gy, WH, ssend.at[2], srecv.at[2])
    start_all(heat_copies)
    wait_sends(temp_copies)
    wait_sends(mat_copies)
    wait_recvs(heat_copies)

    solid_step(s0, s1, cond, heat, 1, SP - 1)
    solid_step(s1, s0, cond, heat, 2, SP - 2)
    solid_step(s0, s1, cond, heat, 3, SP - 3)
    solid_step(s1, s0, cond, heat, 4, SP - 4)

    done = s0[WT : WT + SX, R0 : R0 + SY, :]
    done_b = halves(done.reshape(SLOTS, LN))
    column = lax.broadcasted_iota(I32, (NDEV, SLOTS), 1).astype(F32) + 1.0
    for k in range(CAP):
        hit = onehot(slots_in[:, k : k + 1] == column)
        replies[pl.ds(k, NDEV, stride=CAP), :] = joined(
            jnp.dot(hit, done_b, preferred_element_type=F32)
        )

    def send_back(k, carry):
        px, py = peer_of(gx, gy, (k * 37) & 127)
        other = px * NGY + py
        pltpu.make_async_remote_copy(
            block(replies, other), block(returned, me), a2a_sem.at[4], a2a_sem.at[5],
            device_id=(px, py), device_id_type=MESH,
        ).start()
        return carry

    lax.fori_loop(1, NDEV, send_back, 0)
    own_back = pltpu.make_async_copy(block(replies, me), block(returned, me), self_sem.at[2])
    own_back.start()

    solid_out[...] = done
    wait_sends(faces0)
    wait_sends(heat_copies)

    def sigma(x, carry):
        s1[x, 8 : SR - 8, :] = lookup(mat[x, 8 : SR - 8, :], MODULUS) * s0[x, 8 : SR - 8, :]
        return carry

    lax.fori_loop(WT - 1, WT + SX + 1, sigma, 0)
    lane = lax.broadcasted_iota(I32, (SY, LN), 1)

    def force(x, carry):
        c = s1[x + WT, R0 : R0 + SY, :]
        zp = jnp.where(lane == LN - 1, 0.0, pltpu.roll(c, LN - 1, 1))
        zm = jnp.where(lane == 0, 0.0, pltpu.roll(c, 1, 1))
        stress_out[0, x] = 0.5 * (
            s1[x + WT + 1, R0 : R0 + SY, :] - s1[x + WT - 1, R0 : R0 + SY, :]
        )
        stress_out[1, x] = 0.5 * (
            s1[x + WT, R0 + 1 : R0 + SY + 1, :] - s1[x + WT, R0 - 1 : R0 + SY - 1, :]
        )
        stress_out[2, x] = 0.5 * (zp - zm)
        return carry

    lax.fori_loop(0, SX, force, 0)

    wait_recvs(faces1)
    put_faces(f1, yrecv.at[1])

    def step_two(x, carry):
        fluid_plane(f1, f0, vel, flux, x)
        return carry

    lax.fori_loop(0, CX, step_two, 0)
    stores = [
        pltpu.make_async_copy(
            f0.at[t, interior[0], interior[1], :], fluid_out.at[:, :, pl.ds(t * LN, LN)], out_sem.at[t]
        )
        for t in range(NT)
    ]
    for st in stores:
        st.start()

    place.wait()
    own_back.wait()
    pltpu.make_async_copy(returned.at[pl.ds(0, count)], returned.at[pl.ds(0, count)], a2a_sem.at[5]).wait()

    def unpack(i, carry):
        for j in range(16):
            r = i * 16 + j
            wall_out[pl.ds(r, 1), :] = returned[pl.ds(dest_s[0, r], 1), :]
        return carry

    lax.fori_loop(0, ROWS // 16, unpack, 0)

    wait_sends(faces1)
    pltpu.make_async_copy(meta_out.at[pl.ds(0, NDEV - 1)], meta_out.at[pl.ds(0, NDEV - 1)], a2a_sem.at[0]).wait()
    pltpu.make_async_copy(outgoing.at[pl.ds(0, count)], outgoing.at[pl.ds(0, count)], a2a_sem.at[2]).wait()
    pltpu.make_async_copy(replies.at[pl.ds(0, count)], replies.at[pl.ds(0, count)], a2a_sem.at[4]).wait()
    for st in stores:
        st.wait()


def body(temp_fluid, velocity, wall_old, wall_mask, owner_map, slot_map, temp_solid, material):
    any_spec = pl.BlockSpec(memory_space=pl.ANY)
    vmem_spec = pl.BlockSpec(memory_space=pltpu.VMEM)
    vm = pltpu.VMEM
    padded = (NT, CX + 2, CY + 2 * PADY, LN)
    dma = pltpu.SemaphoreType.DMA
    fluid, wall, solid, stress = pl.pallas_call(
        kernel,
        out_shape=(
            jax.ShapeDtypeStruct((CX, CY, NT * LN), F32),
            jax.ShapeDtypeStruct((ROWS, LN), F32),
            jax.ShapeDtypeStruct((SX, SY, LN), F32),
            jax.ShapeDtypeStruct((3, SX, SY, LN), F32),
        ),
        in_specs=[any_spec] * 8,
        out_specs=(any_spec, vmem_spec, vmem_spec, vmem_spec),
        scratch_shapes=[
            vm(padded, F32), vm(padded, F32), vm((3, CX, CY, NT * LN), BF16),
            vm((CX, CY, LN), F32), vm((CX, CY, LN), I32), vm((ROWS, LN), F32),
            vm((1, ROWS), I32), vm((1, ROWS), I32), vm((1, ROWS), I32), pltpu.SMEM((1, ROWS), I32),
            vm((NDEV * CAP, LN), F32), vm((NDEV * CAP + CAP, LN), F32),
            vm((NDEV * CAP + CAP, LN), F32), vm((NDEV * CAP, LN), F32),
            vm((NDEV, 1, LN), F32), vm((NDEV, 1, LN), F32),
            vm((SP, SR, LN), F32), vm((SP, SR, LN), F32), vm((SP, SR, LN), I32),
            vm((SP, SR, LN), F32), vm((SP, SR, LN), F32),
            vm((2, 2, NT, CX, LN), F32), vm((2, 2, NT, CX, LN), F32),
            dma((16,)), dma((NT,)), dma((3,)), dma((6,)),
            dma((2, 4)), dma((2, 4)), dma((3, 8)), dma((3, 8)),
        ],
        compiler_params=pltpu.CompilerParams(
            collective_id=0, has_side_effects=True, vmem_limit_bytes=60 * 1024 * 1024
        ),
    )(
        temp_fluid, velocity, wall_old, wall_mask,
        owner_map.reshape(1, ROWS), slot_map, temp_solid, material,
    )
    return fluid, wall.reshape(CX, CY, LN), solid, stress


def solution(mesh):
    placed = (
        P("gx", "gy", None),
        P(None, "gx", "gy", None),
        P("gx", "gy", None),
        P("gx", "gy", None),
        P(("gx", "gy"), None, None),
        P(("gx", "gy"), None),
        P("gx", "gy", None),
        P("gx", "gy", None),
    )
    return jax.shard_map(
        body,
        mesh=mesh,
        in_specs=placed,
        out_specs=(
            P("gx", "gy", None),
            P("gx", "gy", None),
            P("gx", "gy", None),
            P(None, "gx", "gy", None),
        ),
        check_vma=False,
    )
```

```python
import functools

import jax
import jax.numpy as jnp
from jax import lax
from jax.experimental import pallas as pl
from jax.experimental.pallas import tpu as pltpu
from jax.sharding import PartitionSpec as P

MESH = pl.DeviceIdType.MESH
F32 = jnp.float32
BF16 = jnp.bfloat16
I32 = jnp.int32

NGX, NGY = 16, 8
NDEV = 128
CX, CY, NT, LN = 16, 64, 8, 128
SX, SY = 16, 32
CAP = 24
ROWS = 1024
SLOTS = 512
PADY = 8
WT = 5
WH = 4
SP = SX + 2 * WT
SR = 64
R0 = 16
CONDUCT = (0.05 * 0.4, 0.05 * 0.9, 0.05 * 1.5, 0.05 * 2.2)
MODULUS = (0.5, 1.0, 1.6, 2.4)
DIRS = [(dx, dy) for dx in (-1, 0, 1) for dy in (-1, 0, 1) if (dx, dy) != (0, 0)]


def peer_of(gx, gy, k):
    dc, dx, dy, dz = k & 1, (k >> 1) & 3, (k >> 3) & 3, (k >> 5) & 3
    c, z, x, y = gx & 1, gx >> 2, gy & 3, (gx & 2) | (gy >> 2)
    nc, nx, ny, nz = c ^ dc, (x + dx) & 3, (y + dy) & 3, (z + dz) & 3
    return (nz << 2) | (ny & 2) | nc, ((ny & 1) << 2) | nx


def halves(value):
    hi = value.astype(BF16)
    lo = (value - hi.astype(F32)).astype(BF16)
    return jnp.concatenate([hi, lo], axis=1)


def joined(product):
    return product[:, :LN] + product[:, LN:]


def onehot(mask):
    return jnp.where(mask, 1.0, 0.0).astype(BF16)


def lookup(material, table):
    out = jnp.where(material == 0, table[0], 0.0)
    for index in range(1, 4):
        out = jnp.where(material == index, table[index], out)
    return out.astype(F32)


def planes(step, width):
    if step > 0:
        return pl.ds(WT + SX - width, width), pl.ds(WT - width, width)
    if step < 0:
        return pl.ds(WT, width), pl.ds(WT + SX, width)
    return pl.ds(WT, SX), pl.ds(WT, SX)


def lines(step):
    if step > 0:
        return pl.ds(R0 + SY - 8, 8), pl.ds(R0 - 8, 8)
    if step < 0:
        return pl.ds(R0, 8), pl.ds(R0 + SY, 8)
    return pl.ds(R0, SY), pl.ds(R0, SY)


def inside(gx, gy, dx, dy):
    px, py = gx + dx, gy + dy
    return (px >= 0) & (px < NGX) & (py >= 0) & (py < NGY)


def spread_copies(ref, gx, gy, width, sends, recvs):
    out = []
    for i, (dx, dy) in enumerate(DIRS):
        xs, xd = planes(dx, width)
        ys, yd = lines(dy)
        copy = pltpu.make_async_remote_copy(
            src_ref=ref.at[xs, ys, :],
            dst_ref=ref.at[xd, yd, :],
            send_sem=sends.at[i],
            recv_sem=recvs.at[i],
            device_id=(gx + dx, gy + dy),
            device_id_type=MESH,
        )
        out.append((copy, inside(gx, gy, dx, dy), inside(gx, gy, -dx, -dy)))
    return out


def start_all(copies):
    for copy, to, _ in copies:
        pl.when(to)(copy.start)


def wait_recvs(copies):
    for copy, _, came in copies:
        pl.when(came)(copy.wait_recv)


def wait_sends(copies):
    for copy, to, _ in copies:
        pl.when(to)(copy.wait_send)


def face_copies(field, ysend, yrecv, gx, gy, sends, recvs):
    out = []
    rows = pl.ds(PADY, CY)
    for i, step in enumerate((1, -1)):
        src, dst = (CX, 0) if step > 0 else (1, CX + 1)
        copy = pltpu.make_async_remote_copy(
            src_ref=field.at[:, src, rows, :],
            dst_ref=field.at[:, dst, rows, :],
            send_sem=sends.at[i],
            recv_sem=recvs.at[i],
            device_id=(gx + step, gy),
            device_id_type=MESH,
        )
        out.append((copy, inside(gx, gy, step, 0), inside(gx, gy, -step, 0)))
    for i, step in enumerate((1, -1)):
        copy = pltpu.make_async_remote_copy(
            src_ref=ysend.at[i],
            dst_ref=yrecv.at[i],
            send_sem=sends.at[2 + i],
            recv_sem=recvs.at[2 + i],
            device_id=(gx, gy + step),
            device_id_type=MESH,
        )
        out.append((copy, inside(gx, gy, 0, step), inside(gx, gy, 0, -step)))
    return out


def take_faces(field, ysend):
    for t in range(NT):
        ysend[0, t] = field[t, 1 : CX + 1, PADY + CY - 1, :]
        ysend[1, t] = field[t, 1 : CX + 1, PADY, :]


def put_faces(field, yrecv):
    for t in range(NT):
        field[t, 1 : CX + 1, PADY - 1, :] = yrecv[0, t]
        field[t, 1 : CX + 1, PADY + CY, :] = yrecv[1, t]


def fluid_plane(src, put, vel, flux, x):
    lane = lax.broadcasted_iota(I32, (16, LN), 1)
    first, last = lane == 0, lane == LN - 1
    zero = jnp.zeros((16, LN), F32)
    for h in range(CY // 16):
        r = PADY + 16 * h
        mids = [src[t, x + 1, r : r + 16, :] for t in range(NT)]
        ups = [pltpu.roll(c, LN - 1, 1) for c in mids] + [zero]
        downs = [zero] + [pltpu.roll(c, 1, 1) for c in mids]
        for t in range(NT):
            c = mids[t]
            pairs = (
                (src[t, x + 2, r : r + 16, :], src[t, x, r : r + 16, :]),
                (src[t, x + 1, r + 1 : r + 17, :], src[t, x + 1, r - 1 : r + 15, :]),
                (jnp.where(last, ups[t + 1], ups[t]), jnp.where(first, downs[t], downs[t + 1])),
            )
            total = None
            for k, (p, m) in enumerate(pairs):
                u = vel[k, x, 16 * h : 16 * h + 16, t * LN : (t + 1) * LN].astype(F32)
                a = jnp.maximum(u + 0.5, 0.5)
                pc = p - c
                term = a * ((m - c) + pc) - u * pc
                total = term if total is None else total + term
            if t == 0:
                total = total - flux[pl.ds(pl.multiple_of(x * CY + 16 * h, 16), 16), :]
            put(t, x, h, c + 0.1 * total)


def solid_step(src, dst, cond, heat):
    lane = lax.broadcasted_iota(I32, (SR - 16, LN), 1)
    last, first = lane == LN - 1, lane == 0
    for x in range(1, SP - 1):
        c = src[x, 8 : SR - 8, :]
        zp = jnp.where(last, 0.0, pltpu.roll(c, LN - 1, 1))
        zm = jnp.where(first, 0.0, pltpu.roll(c, 1, 1))
        beside = src[x + 1, 8 : SR - 8, :] + src[x - 1, 8 : SR - 8, :]
        beside = beside + (src[x, 9 : SR - 7, :] + src[x, 7 : SR - 9, :])
        lap = beside + (zp + zm) - 6.0 * c
        dst[x, 8 : SR - 8, :] = c + (cond[x, 8 : SR - 8, :] * lap + 0.2 * heat[x, 8 : SR - 8, :])


def kernel(
    fluid_in, vel_in, wall_in, mask_in, owner_in, slot_in, solid_in, mat_in,
    fluid_out, wall_out, solid_out, stress_out,
    f0, f1, vel, wall, mask, flux, owner, slot, dest, dest_s,
    outgoing, incoming, replies, returned, meta_out, meta_in,
    s0, s1, mat, cond, heat, ysend, yrecv,
    in_sem, self_sem, a2a_sem, fsend, frecv, ssend, srecv,
):
    gx, gy = lax.axis_index("gx"), lax.axis_index("gy")
    me = gx * NGY + gy

    loads = [
        pltpu.make_async_copy(owner_in, owner, in_sem.at[0]),
        pltpu.make_async_copy(slot_in, slot, in_sem.at[1]),
        pltpu.make_async_copy(wall_in, wall, in_sem.at[2]),
        pltpu.make_async_copy(mask_in, mask, in_sem.at[3]),
    ]
    interior = (pl.ds(1, CX), pl.ds(PADY, CY))
    tiles = [
        pltpu.make_async_copy(
            fluid_in.at[:, :, pl.ds(t * LN, LN)], f0.at[t, interior[0], interior[1], :], in_sem.at[4 + t]
        )
        for t in range(NT)
    ]
    core = (pl.ds(WT, SX), pl.ds(R0, SY))
    load_solid = pltpu.make_async_copy(solid_in, s0.at[core[0], core[1], :], in_sem.at[12])
    load_mat = pltpu.make_async_copy(mat_in, mat.at[core[0], core[1], :], in_sem.at[13])
    load_vel = pltpu.make_async_copy(vel_in, vel, in_sem.at[14])

    for ld in loads[:2]:
        ld.start()
    tiles[0].start()
    for ld in loads[2:]:
        ld.start()

    for field in (f0, f1):
        for t in range(NT):
            for x in (0, CX + 1):
                field[t, x] = jnp.zeros((CY + 2 * PADY, LN), F32)
    yrecv[...] = jnp.zeros_like(yrecv)

    def clear(x, carry):
        for ref, value in ((s0, 0.0), (heat, 0.0), (mat, -1)):
            ref[x, 8:R0, :] = jnp.full((8, LN), value, ref.dtype)
            ref[x, R0 + SY : R0 + SY + 8, :] = jnp.full((8, LN), value, ref.dtype)
        return carry

    lax.fori_loop(0, SP, clear, 0)
    for x in list(range(WT)) + list(range(WT + SX, SP)):
        for ref, value in ((s0, 0.0), (heat, 0.0), (mat, -1)):
            ref[x, R0 : R0 + SY, :] = jnp.full((SY, LN), value, ref.dtype)

    barrier = pltpu.get_barrier_semaphore()

    def greet(k, carry):
        px, py = peer_of(gx, gy, (k * 37) & 127)
        pl.semaphore_signal(barrier, inc=1, device_id=(px, py), device_id_type=MESH)
        return carry

    lax.fori_loop(1, NDEV, greet, 0)
    load_solid.start()
    load_mat.start()
    for t in range(1, NT):
        tiles[t].start()
    load_vel.start()

    loads[0].wait()
    loads[1].wait()
    own_row = owner[...]
    mine = own_row == lax.broadcasted_iota(I32, (NDEV, ROWS), 0)
    mine_b = onehot(mine)
    before = onehot(
        lax.broadcasted_iota(I32, (ROWS, ROWS), 0) < lax.broadcasted_iota(I32, (ROWS, ROWS), 1)
    )
    ranks = jnp.dot(mine_b, before, preferred_element_type=F32)
    rank_row = jnp.sum(jnp.where(mine, ranks, 0.0), axis=0, keepdims=True).astype(I32)
    dest[...] = jnp.clip(own_row * CAP + rank_row, 0, NDEV * CAP - 1)
    place = pltpu.make_async_copy(dest, dest_s, in_sem.at[15])
    place.start()
    code = slot[...] + 1
    at_rank = onehot(rank_row == lax.broadcasted_iota(I32, (LN, ROWS), 0))
    parts = []
    for part in (code & 15, code >> 4):
        left = jnp.where(mine, part.astype(F32), 0.0).astype(BF16)
        parts.append(
            lax.dot_general(left, at_rank, (((1,), (1,)), ((), ())), preferred_element_type=F32)
        )
    meta_out[...] = (parts[0] + 16.0 * parts[1]).reshape(NDEV, 1, LN)

    for ld in loads[2:]:
        ld.wait()
    tiles[0].wait()
    for x in range(CX):
        t0 = f0[0, x + 1, PADY : PADY + CY, :]
        flux[x * CY : (x + 1) * CY, :] = mask[x].astype(F32) * 2.0 * (t0 - wall[x])
    flux_b = halves(flux[...])
    chunk = 16 * CAP

    def pack(i, carry):
        base = pl.multiple_of(i * chunk, chunk)
        pick = onehot(dest[...] == lax.broadcasted_iota(I32, (chunk, ROWS), 0) + base)
        outgoing[pl.ds(base, chunk), :] = joined(jnp.dot(pick, flux_b, preferred_element_type=F32))
        return carry

    lax.fori_loop(0, NDEV // 16, pack, 0)

    for t in range(1, NT):
        tiles[t].wait()
    take_faces(f0, ysend.at[0])
    faces0 = face_copies(f0, ysend.at[0], yrecv.at[0], gx, gy, fsend.at[0], frecv.at[0])
    pl.semaphore_wait(barrier, NDEV - 1)
    start_all(faces0)

    def block(ref, d):
        return ref.at[pl.ds(pl.multiple_of(d * CAP, CAP), CAP), :]

    def send_rows(k, carry):
        px, py = peer_of(gx, gy, (k * 37) & 127)
        other = px * NGY + py
        pltpu.make_async_remote_copy(
            meta_out.at[other], meta_in.at[me], a2a_sem.at[0], a2a_sem.at[1],
            device_id=(px, py), device_id_type=MESH,
        ).start()
        pltpu.make_async_remote_copy(
            block(outgoing, other), block(incoming, me), a2a_sem.at[2], a2a_sem.at[3],
            device_id=(px, py), device_id_type=MESH,
        ).start()
        return carry

    lax.fori_loop(1, NDEV, send_rows, 0)
    own_meta = pltpu.make_async_copy(meta_out.at[me], meta_in.at[me], self_sem.at[0])
    own_rows = pltpu.make_async_copy(block(outgoing, me), block(incoming, me), self_sem.at[1])
    own_meta.start()
    own_rows.start()

    load_solid.wait()
    load_mat.wait()
    temp_copies = spread_copies(s0, gx, gy, WT, ssend.at[0], srecv.at[0])
    mat_copies = spread_copies(mat, gx, gy, WT, ssend.at[1], srecv.at[1])
    start_all(temp_copies)
    start_all(mat_copies)

    load_vel.wait()
    wait_recvs(faces0)
    put_faces(f0, yrecv.at[0])

    def keep(t, x, h, value):
        f1[t, x + 1, PADY + 16 * h : PADY + 16 * h + 16, :] = value

    def step_one(x, carry):
        fluid_plane(f0, keep, vel, flux, x)
        return carry

    lax.fori_loop(0, CX, step_one, 0)

    take_faces(f1, ysend.at[1])
    faces1 = face_copies(f1, ysend.at[1], yrecv.at[1], gx, gy, fsend.at[1], frecv.at[1])

    wait_recvs(temp_copies)
    wait_recvs(mat_copies)

    def conduct(x, carry):
        for j in range(2):
            cond[2 * x + j, 8 : SR - 8, :] = lookup(mat[2 * x + j, 8 : SR - 8, :], CONDUCT)
        return carry

    lax.fori_loop(0, SP // 2, conduct, 0)

    count = (NDEV - 1) * CAP
    own_meta.wait()
    own_rows.wait()
    pltpu.make_async_copy(meta_in.at[pl.ds(0, NDEV - 1)], meta_in.at[pl.ds(0, NDEV - 1)], a2a_sem.at[1]).wait()
    pltpu.make_async_copy(incoming.at[pl.ds(0, count)], incoming.at[pl.ds(0, count)], a2a_sem.at[3]).wait()
    start_all(faces1)
    slots_in = meta_in[...].reshape(NDEV, LN)
    slots_t = slots_in.T
    wanted = lax.broadcasted_iota(I32, (SLOTS, NDEV), 0).astype(F32) + 1.0
    total = None
    for first in range(0, CAP, 6):
        span = range(first, first + 6)
        hits = jnp.concatenate([onehot(slots_t[k : k + 1, :] == wanted) for k in span], axis=1)
        rows = jnp.concatenate(
            [halves(incoming[pl.ds(k, NDEV, stride=CAP), :]) for k in span], axis=0
        )
        some = jnp.dot(hits, rows, preferred_element_type=F32)
        total = some if total is None else total + some
    heat[WT : WT + SX, R0 : R0 + SY, :] = joined(total).reshape(SX, SY, LN)
    heat_copies = spread_copies(heat, gx, gy, WH, ssend.at[2], srecv.at[2])
    start_all(heat_copies)
    wait_sends(temp_copies)
    wait_sends(mat_copies)
    wait_recvs(heat_copies)

    solid_step(s0, s1, cond, heat)
    solid_step(s1, s0, cond, heat)
    solid_step(s0, s1, cond, heat)
    solid_step(s1, s0, cond, heat)

    done = s0[WT : WT + SX, R0 : R0 + SY, :]
    done_b = halves(done.reshape(SLOTS, LN))
    part = NDEV // 4
    column = lax.broadcasted_iota(I32, (part, SLOTS), 1).astype(F32) + 1.0
    for q in range(4):
        dz = (gx >> 2) + q
        first = pl.multiple_of((dz & 3) * part, part)
        some_slots = meta_in[pl.ds(first, part)].reshape(part, LN)
        hits = jnp.concatenate(
            [onehot(some_slots[:, k : k + 1] == column) for k in range(CAP)], axis=0
        )
        picked = joined(jnp.dot(hits, done_b, preferred_element_type=F32))
        for k in range(CAP):
            replies[pl.ds(first * CAP + k, part, stride=CAP), :] = picked[k * part : (k + 1) * part]

        def send_back(k, carry):
            px, py = peer_of(gx, gy, q * 32 + ((k * 13) & 31))
            other = px * NGY + py
            pltpu.make_async_remote_copy(
                block(replies, other), block(returned, me), a2a_sem.at[4], a2a_sem.at[5],
                device_id=(px, py), device_id_type=MESH,
            ).start()
            return carry

        lax.fori_loop(1 if q == 0 else 0, 32, send_back, 0)
    own_back = pltpu.make_async_copy(block(replies, me), block(returned, me), self_sem.at[2])
    own_back.start()

    solid_out[...] = done
    wait_sends(faces0)
    wait_sends(heat_copies)

    def sigma(x, carry):
        for j in range(2):
            y = WT - 1 + 2 * x + j
            s1[y, 8 : SR - 8, :] = lookup(mat[y, 8 : SR - 8, :], MODULUS) * s0[y, 8 : SR - 8, :]
        return carry

    lax.fori_loop(0, SX // 2 + 1, sigma, 0)
    lane = lax.broadcasted_iota(I32, (SY, LN), 1)

    def force(x, carry):
        c = s1[x + WT, R0 : R0 + SY, :]
        zp = jnp.where(lane == LN - 1, 0.0, pltpu.roll(c, LN - 1, 1))
        zm = jnp.where(lane == 0, 0.0, pltpu.roll(c, 1, 1))
        stress_out[0, x] = 0.5 * (
            s1[x + WT + 1, R0 : R0 + SY, :] - s1[x + WT - 1, R0 : R0 + SY, :]
        )
        stress_out[1, x] = 0.5 * (
            s1[x + WT, R0 + 1 : R0 + SY + 1, :] - s1[x + WT, R0 - 1 : R0 + SY - 1, :]
        )
        stress_out[2, x] = 0.5 * (zp - zm)
        return carry

    lax.fori_loop(0, SX, force, 0)

    wait_recvs(faces1)
    put_faces(f1, yrecv.at[1])

    def give(t, x, h, value):
        fluid_out[x, 16 * h : 16 * h + 16, t * LN : (t + 1) * LN] = value

    def step_two(x, carry):
        fluid_plane(f1, give, vel, flux, x)
        return carry

    lax.fori_loop(0, CX, step_two, 0)

    place.wait()
    own_back.wait()
    pltpu.make_async_copy(returned.at[pl.ds(0, count)], returned.at[pl.ds(0, count)], a2a_sem.at[5]).wait()

    def unpack(i, carry):
        for j in range(16):
            r = i * 16 + j
            wall_out[pl.ds(r, 1), :] = returned[pl.ds(dest_s[0, r], 1), :]
        return carry

    lax.fori_loop(0, ROWS // 16, unpack, 0)

    wait_sends(faces1)
    pltpu.make_async_copy(meta_out.at[pl.ds(0, NDEV - 1)], meta_out.at[pl.ds(0, NDEV - 1)], a2a_sem.at[0]).wait()
    pltpu.make_async_copy(outgoing.at[pl.ds(0, count)], outgoing.at[pl.ds(0, count)], a2a_sem.at[2]).wait()
    pltpu.make_async_copy(replies.at[pl.ds(0, count)], replies.at[pl.ds(0, count)], a2a_sem.at[4]).wait()


def store(*refs):
    sems = refs[-1]
    copies = [pltpu.make_async_copy(refs[i], refs[4 + i], sems.at[i]) for i in range(4)]
    for copy in copies:
        copy.start()
    for copy in copies:
        copy.wait()


def body(temp_fluid, velocity, wall_old, wall_mask, owner_map, slot_map, temp_solid, material):
    hbm_spec = pl.BlockSpec(memory_space=pltpu.HBM)
    vmem_spec = pl.BlockSpec(memory_space=pltpu.VMEM)
    vm = pltpu.VMEM
    padded = (NT, CX + 2, CY + 2 * PADY, LN)
    dma = pltpu.SemaphoreType.DMA
    fluid, wall, solid, stress = pl.pallas_call(
        kernel,
        out_shape=(
            jax.ShapeDtypeStruct((CX, CY, NT * LN), F32),
            jax.ShapeDtypeStruct((ROWS, LN), F32),
            jax.ShapeDtypeStruct((SX, SY, LN), F32),
            jax.ShapeDtypeStruct((3, SX, SY, LN), F32),
        ),
        in_specs=[hbm_spec] * 8,
        out_specs=(vmem_spec,) * 4,
        scratch_shapes=[
            vm(padded, F32), vm(padded, F32), vm((3, CX, CY, NT * LN), BF16),
            vm((CX, CY, LN), F32), vm((CX, CY, LN), I32), vm((ROWS, LN), F32),
            vm((1, ROWS), I32), vm((1, ROWS), I32), vm((1, ROWS), I32), pltpu.SMEM((1, ROWS), I32),
            vm((NDEV * CAP, LN), F32), vm((NDEV * CAP + CAP, LN), F32),
            vm((NDEV * CAP + CAP, LN), F32), vm((NDEV * CAP, LN), F32),
            vm((NDEV, 1, LN), F32), vm((NDEV, 1, LN), F32),
            vm((SP, SR, LN), F32), vm((SP, SR, LN), F32), vm((SP, SR, LN), I32),
            vm((SP, SR, LN), F32), vm((SP, SR, LN), F32),
            vm((2, 2, NT, CX, LN), F32), vm((2, 2, NT, CX, LN), F32),
            dma((16,)), dma((3,)), dma((10,)),
            dma((2, 4)), dma((2, 4)), dma((3, 8)), dma((3, 8)),
        ],
        compiler_params=pltpu.CompilerParams(
            collective_id=0, has_side_effects=True, vmem_limit_bytes=40 * 1024 * 1024
        ),
    )(*[
        pltpu.with_memory_space_constraint(x, pltpu.HBM)
        for x in (temp_fluid, velocity, wall_old, wall_mask,
        owner_map.reshape(1, ROWS), slot_map, temp_solid, material)
    ])
    results = (fluid, wall.reshape(CX, CY, LN), solid, stress)
    return pl.pallas_call(
        store,
        out_shape=tuple(jax.ShapeDtypeStruct(r.shape, F32) for r in results),
        in_specs=[pl.BlockSpec(memory_space=pl.ANY)] * 4,
        out_specs=(pl.BlockSpec(memory_space=pl.ANY),) * 4,
        scratch_shapes=[dma((4,))],
        compiler_params=pltpu.CompilerParams(vmem_limit_bytes=1024 * 1024),
    )(*results)


def solution(mesh):
    placed = (
        P("gx", "gy", None),
        P(None, "gx", "gy", None),
        P("gx", "gy", None),
        P("gx", "gy", None),
        P(("gx", "gy"), None, None),
        P(("gx", "gy"), None),
        P("gx", "gy", None),
        P("gx", "gy", None),
    )
    return jax.shard_map(
        body,
        mesh=mesh,
        in_specs=placed,
        out_specs=(
            P("gx", "gy", None),
            P("gx", "gy", None),
            P("gx", "gy", None),
            P(None, "gx", "gy", None),
        ),
        check_vma=False,
    )
```

```python
import functools

import jax
import jax.numpy as jnp
from jax import lax
from jax.experimental import pallas as pl
from jax.experimental.pallas import tpu as pltpu
from jax.sharding import PartitionSpec as P

MESH = pl.DeviceIdType.MESH
F32 = jnp.float32
BF16 = jnp.bfloat16
I32 = jnp.int32

NGX, NGY = 16, 8
NDEV = 128
CX, CY, NT, LN = 16, 64, 8, 128
SX, SY = 16, 32
CAP = 24
ROWS = 1024
SLOTS = 512
PADY = 8
WT = 5
WH = 4
SP = SX + 2 * WT
SR = 64
R0 = 16
CONDUCT = (0.05 * 0.4, 0.05 * 0.9, 0.05 * 1.5, 0.05 * 2.2)
MODULUS = (0.5, 1.0, 1.6, 2.4)
DIRS = [(dx, dy) for dx in (-1, 0, 1) for dy in (-1, 0, 1) if (dx, dy) != (0, 0)]


def peer_of(gx, gy, k):
    dc, dx, dy, dz = k & 1, (k >> 1) & 3, (k >> 3) & 3, (k >> 5) & 3
    c, z, x, y = gx & 1, gx >> 2, gy & 3, (gx & 2) | (gy >> 2)
    nc, nx, ny, nz = c ^ dc, (x + dx) & 3, (y + dy) & 3, (z + dz) & 3
    return (nz << 2) | (ny & 2) | nc, ((ny & 1) << 2) | nx


def halves(value):
    hi = value.astype(BF16)
    lo = (value - hi.astype(F32)).astype(BF16)
    return jnp.concatenate([hi, lo], axis=1)


def joined(product):
    return product[:, :LN] + product[:, LN:]


def onehot(mask):
    return jnp.where(mask, 1.0, 0.0).astype(BF16)


def lookup(material, table):
    out = jnp.where(material == 0, table[0], 0.0)
    for index in range(1, 4):
        out = jnp.where(material == index, table[index], out)
    return out.astype(F32)


def planes(step, width):
    if step > 0:
        return pl.ds(WT + SX - width, width), pl.ds(WT - width, width)
    if step < 0:
        return pl.ds(WT, width), pl.ds(WT + SX, width)
    return pl.ds(WT, SX), pl.ds(WT, SX)


def lines(step):
    if step > 0:
        return pl.ds(R0 + SY - 8, 8), pl.ds(R0 - 8, 8)
    if step < 0:
        return pl.ds(R0, 8), pl.ds(R0 + SY, 8)
    return pl.ds(R0, SY), pl.ds(R0, SY)


def inside(gx, gy, dx, dy):
    px, py = gx + dx, gy + dy
    return (px >= 0) & (px < NGX) & (py >= 0) & (py < NGY)


def spread_copies(ref, gx, gy, width, sends, recvs):
    out = []
    for i, (dx, dy) in enumerate(DIRS):
        xs, xd = planes(dx, width - 1 if dy else width)
        ys, yd = lines(dy)
        copy = pltpu.make_async_remote_copy(
            src_ref=ref.at[xs, ys, :],
            dst_ref=ref.at[xd, yd, :],
            send_sem=sends.at[i],
            recv_sem=recvs.at[i],
            device_id=(gx + dx, gy + dy),
            device_id_type=MESH,
        )
        out.append((copy, inside(gx, gy, dx, dy), inside(gx, gy, -dx, -dy)))
    return out


def start_all(copies):
    for copy, to, _ in copies:
        pl.when(to)(copy.start)


def wait_recvs(copies):
    for copy, _, came in copies:
        pl.when(came)(copy.wait_recv)


def wait_sends(copies):
    for copy, to, _ in copies:
        pl.when(to)(copy.wait_send)


def face_copies(field, ysend, yrecv, gx, gy, sends, recvs):
    out = []
    rows = pl.ds(PADY, CY)
    for i, step in enumerate((1, -1)):
        src, dst = (CX, 0) if step > 0 else (1, CX + 1)
        copy = pltpu.make_async_remote_copy(
            src_ref=field.at[:, src, rows, :],
            dst_ref=field.at[:, dst, rows, :],
            send_sem=sends.at[i],
            recv_sem=recvs.at[i],
            device_id=(gx + step, gy),
            device_id_type=MESH,
        )
        out.append((copy, inside(gx, gy, step, 0), inside(gx, gy, -step, 0)))
    for i, step in enumerate((1, -1)):
        copy = pltpu.make_async_remote_copy(
            src_ref=ysend.at[i],
            dst_ref=yrecv.at[i],
            send_sem=sends.at[2 + i],
            recv_sem=recvs.at[2 + i],
            device_id=(gx, gy + step),
            device_id_type=MESH,
        )
        out.append((copy, inside(gx, gy, 0, step), inside(gx, gy, 0, -step)))
    return out


def take_faces(field, ysend):
    for t in range(NT):
        ysend[0, t] = field[t, 1 : CX + 1, PADY + CY - 1, :]
        ysend[1, t] = field[t, 1 : CX + 1, PADY, :]


def put_faces(field, yrecv):
    for t in range(NT):
        field[t, 1 : CX + 1, PADY - 1, :] = yrecv[0, t]
        field[t, 1 : CX + 1, PADY + CY, :] = yrecv[1, t]


def fluid_plane(src, put, vel, flux, x):
    lane = lax.broadcasted_iota(I32, (16, LN), 1)
    first, last = lane == 0, lane == LN - 1
    zero = jnp.zeros((16, LN), F32)
    for h in range(CY // 16):
        r = PADY + 16 * h
        mids = [src[t, x + 1, r : r + 16, :] for t in range(NT)]
        ups = [pltpu.roll(c, LN - 1, 1) for c in mids] + [zero]
        downs = [zero] + [pltpu.roll(c, 1, 1) for c in mids]
        for t in range(NT):
            c = mids[t]
            pairs = (
                (src[t, x + 2, r : r + 16, :], src[t, x, r : r + 16, :]),
                (src[t, x + 1, r + 1 : r + 17, :], src[t, x + 1, r - 1 : r + 15, :]),
                (jnp.where(last, ups[t + 1], ups[t]), jnp.where(first, downs[t], downs[t + 1])),
            )
            total = None
            for k, (p, m) in enumerate(pairs):
                u = vel[k, x, 16 * h : 16 * h + 16, t * LN : (t + 1) * LN].astype(F32)
                a = jnp.maximum(u + 0.5, 0.5)
                pc = p - c
                term = a * ((m - c) + pc) - u * pc
                total = term if total is None else total + term
            if t == 0:
                total = total - flux[pl.ds(pl.multiple_of(x * CY + 16 * h, 16), 16), :]
            put(t, x, h, c + 0.1 * total)


def solid_step(src, dst, cond, heat):
    lane = lax.broadcasted_iota(I32, (SR - 16, LN), 1)
    last, first = lane == LN - 1, lane == 0
    for x in range(1, SP - 1):
        c = src[x, 8 : SR - 8, :]
        zp = jnp.where(last, 0.0, pltpu.roll(c, LN - 1, 1))
        zm = jnp.where(first, 0.0, pltpu.roll(c, 1, 1))
        beside = src[x + 1, 8 : SR - 8, :] + src[x - 1, 8 : SR - 8, :]
        beside = beside + (src[x, 9 : SR - 7, :] + src[x, 7 : SR - 9, :])
        lap = beside + (zp + zm) - 6.0 * c
        dst[x, 8 : SR - 8, :] = c + (cond[x, 8 : SR - 8, :] * lap + 0.2 * heat[x, 8 : SR - 8, :])


def kernel(
    fluid_in, vel_in, wall_in, mask_in, owner_in, slot_in, solid_in, mat_in,
    fluid_out, wall_out, solid_out, stress_out,
    f0, f1, vel, wall, mask, flux, owner, slot, dest, dest_s,
    outgoing, incoming, replies, returned, meta_out, meta_in,
    s0, s1, mat, cond, heat, ysend, yrecv,
    in_sem, self_sem, a2a_sem, fsend, frecv, ssend, srecv,
):
    gx, gy = lax.axis_index("gx"), lax.axis_index("gy")
    me = gx * NGY + gy

    loads = [
        pltpu.make_async_copy(owner_in, owner, in_sem.at[0]),
        pltpu.make_async_copy(slot_in, slot, in_sem.at[1]),
        pltpu.make_async_copy(wall_in, wall, in_sem.at[2]),
        pltpu.make_async_copy(mask_in, mask, in_sem.at[3]),
    ]
    interior = (pl.ds(1, CX), pl.ds(PADY, CY))
    tiles = [
        pltpu.make_async_copy(
            fluid_in.at[:, :, pl.ds(t * LN, LN)], f0.at[t, interior[0], interior[1], :], in_sem.at[4 + t]
        )
        for t in range(NT)
    ]
    core = (pl.ds(WT, SX), pl.ds(R0, SY))
    load_solid = pltpu.make_async_copy(solid_in, s0.at[core[0], core[1], :], in_sem.at[12])
    load_mat = pltpu.make_async_copy(mat_in, mat.at[core[0], core[1], :], in_sem.at[13])
    load_vel = pltpu.make_async_copy(vel_in, vel, in_sem.at[14])

    for ld in loads[:2]:
        ld.start()
    tiles[0].start()
    for ld in loads[2:]:
        ld.start()

    for field in (f0, f1):
        for t in range(NT):
            for x in (0, CX + 1):
                field[t, x] = jnp.zeros((CY + 2 * PADY, LN), F32)
    yrecv[...] = jnp.zeros_like(yrecv)

    def clear(x, carry):
        for ref, value in ((s0, 0.0), (heat, 0.0), (mat, -1)):
            ref[x, 8:R0, :] = jnp.full((8, LN), value, ref.dtype)
            ref[x, R0 + SY : R0 + SY + 8, :] = jnp.full((8, LN), value, ref.dtype)
        return carry

    lax.fori_loop(0, SP, clear, 0)
    for x in list(range(WT)) + list(range(WT + SX, SP)):
        for ref, value in ((s0, 0.0), (heat, 0.0), (mat, -1)):
            ref[x, R0 : R0 + SY, :] = jnp.full((SY, LN), value, ref.dtype)

    barrier = pltpu.get_barrier_semaphore()

    def greet(k, carry):
        px, py = peer_of(gx, gy, (k * 37) & 127)
        pl.semaphore_signal(barrier, inc=1, device_id=(px, py), device_id_type=MESH)
        return carry

    lax.fori_loop(1, NDEV, greet, 0)
    load_solid.start()
    load_mat.start()
    for t in range(1, NT):
        tiles[t].start()
    load_vel.start()

    loads[0].wait()
    loads[1].wait()
    own_row = owner[...]
    mine = own_row == lax.broadcasted_iota(I32, (NDEV, ROWS), 0)
    mine_b = onehot(mine)
    before = onehot(
        lax.broadcasted_iota(I32, (ROWS, ROWS), 0) < lax.broadcasted_iota(I32, (ROWS, ROWS), 1)
    )
    ranks = jnp.dot(mine_b, before, preferred_element_type=F32)
    rank_row = jnp.sum(jnp.where(mine, ranks, 0.0), axis=0, keepdims=True).astype(I32)
    dest[...] = jnp.clip(own_row * CAP + rank_row, 0, NDEV * CAP - 1)
    place = pltpu.make_async_copy(dest, dest_s, in_sem.at[15])
    place.start()
    code = slot[...] + 1
    at_rank = onehot(rank_row == lax.broadcasted_iota(I32, (LN, ROWS), 0))
    parts = []
    for part in (code & 15, code >> 4):
        left = jnp.where(mine, part.astype(F32), 0.0).astype(BF16)
        parts.append(
            lax.dot_general(left, at_rank, (((1,), (1,)), ((), ())), preferred_element_type=F32)
        )
    meta_out[...] = (parts[0] + 16.0 * parts[1]).reshape(NDEV, 1, LN)

    for ld in loads[2:]:
        ld.wait()
    tiles[0].wait()
    for x in range(CX):
        t0 = f0[0, x + 1, PADY : PADY + CY, :]
        flux[x * CY : (x + 1) * CY, :] = mask[x].astype(F32) * 2.0 * (t0 - wall[x])
    flux_b = halves(flux[...])
    chunk = 16 * CAP

    def pack(i, carry):
        base = pl.multiple_of(i * chunk, chunk)
        pick = onehot(dest[...] == lax.broadcasted_iota(I32, (chunk, ROWS), 0) + base)
        outgoing[pl.ds(base, chunk), :] = joined(jnp.dot(pick, flux_b, preferred_element_type=F32))
        return carry

    lax.fori_loop(0, NDEV // 16, pack, 0)

    for t in range(1, NT):
        tiles[t].wait()
    take_faces(f0, ysend.at[0])
    faces0 = face_copies(f0, ysend.at[0], yrecv.at[0], gx, gy, fsend.at[0], frecv.at[0])
    pl.semaphore_wait(barrier, NDEV - 1)
    start_all(faces0)

    def block(ref, d):
        return ref.at[pl.ds(pl.multiple_of(d * CAP, CAP), CAP), :]

    def send_rows(k, carry):
        px, py = peer_of(gx, gy, (k * 37) & 127)
        other = px * NGY + py
        pltpu.make_async_remote_copy(
            meta_out.at[other], meta_in.at[me], a2a_sem.at[0], a2a_sem.at[1],
            device_id=(px, py), device_id_type=MESH,
        ).start()
        pltpu.make_async_remote_copy(
            block(outgoing, other), block(incoming, me), a2a_sem.at[2], a2a_sem.at[3],
            device_id=(px, py), device_id_type=MESH,
        ).start()
        return carry

    lax.fori_loop(1, NDEV, send_rows, 0)
    own_meta = pltpu.make_async_copy(meta_out.at[me], meta_in.at[me], self_sem.at[0])
    own_rows = pltpu.make_async_copy(block(outgoing, me), block(incoming, me), self_sem.at[1])
    own_meta.start()
    own_rows.start()

    load_solid.wait()
    load_mat.wait()
    temp_copies = spread_copies(s0, gx, gy, WT, ssend.at[0], srecv.at[0])
    mat_copies = spread_copies(mat, gx, gy, WH, ssend.at[1], srecv.at[1])
    start_all(temp_copies)
    start_all(mat_copies)

    load_vel.wait()
    wait_recvs(faces0)
    put_faces(f0, yrecv.at[0])

    def keep(t, x, h, value):
        f1[t, x + 1, PADY + 16 * h : PADY + 16 * h + 16, :] = value

    def step_one(x, carry):
        fluid_plane(f0, keep, vel, flux, x)
        return carry

    lax.fori_loop(0, CX, step_one, 0)

    take_faces(f1, ysend.at[1])
    faces1 = face_copies(f1, ysend.at[1], yrecv.at[1], gx, gy, fsend.at[1], frecv.at[1])

    count = (NDEV - 1) * CAP
    own_meta.wait()
    own_rows.wait()
    pltpu.make_async_copy(meta_in.at[pl.ds(0, NDEV - 1)], meta_in.at[pl.ds(0, NDEV - 1)], a2a_sem.at[1]).wait()
    pltpu.make_async_copy(incoming.at[pl.ds(0, count)], incoming.at[pl.ds(0, count)], a2a_sem.at[3]).wait()
    slots_in = meta_in[...].reshape(NDEV, LN)
    slots_t = slots_in.T
    wanted = lax.broadcasted_iota(I32, (SLOTS, NDEV), 0).astype(F32) + 1.0
    total = None
    for first in range(0, CAP, 6):
        span = range(first, first + 6)
        hits = jnp.concatenate([onehot(slots_t[k : k + 1, :] == wanted) for k in span], axis=1)
        rows = jnp.concatenate(
            [halves(incoming[pl.ds(k, NDEV, stride=CAP), :]) for k in span], axis=0
        )
        some = jnp.dot(hits, rows, preferred_element_type=F32)
        total = some if total is None else total + some
    heat[WT : WT + SX, R0 : R0 + SY, :] = joined(total).reshape(SX, SY, LN)
    heat_copies = spread_copies(heat, gx, gy, WH, ssend.at[2], srecv.at[2])
    start_all(heat_copies)
    start_all(faces1)
    wait_recvs(temp_copies)
    wait_recvs(mat_copies)

    def conduct(x, carry):
        for j in range(2):
            cond[2 * x + j, 8 : SR - 8, :] = lookup(mat[2 * x + j, 8 : SR - 8, :], CONDUCT)
        return carry

    lax.fori_loop(0, SP // 2, conduct, 0)

    wait_sends(temp_copies)
    wait_sends(mat_copies)
    wait_recvs(heat_copies)

    solid_step(s0, s1, cond, heat)
    solid_step(s1, s0, cond, heat)
    solid_step(s0, s1, cond, heat)
    solid_step(s1, s0, cond, heat)

    done = s0[WT : WT + SX, R0 : R0 + SY, :]
    done_b = halves(done.reshape(SLOTS, LN))
    column = lax.broadcasted_iota(I32, (NDEV // 2, SLOTS), 1).astype(F32) + 1.0
    for core in range(2):
        starts = [(2 * g + core) * NGY for g in range(NGX // 2)]
        some_slots = jnp.concatenate(
            [meta_in[b : b + NGY].reshape(NGY, LN) for b in starts], axis=0
        )
        hits = jnp.concatenate(
            [onehot(some_slots[:, k : k + 1] == column) for k in range(CAP)], axis=0
        )
        picked = joined(jnp.dot(hits, done_b, preferred_element_type=F32))
        for k in range(CAP):
            for g, b in enumerate(starts):
                r = k * (NDEV // 2) + g * NGY
                replies[pl.ds(b * CAP + k, NGY, stride=CAP), :] = picked[r : r + NGY]
        flip = (gx & 1) ^ core

        def send_back(j, carry):
            px, py = peer_of(gx, gy, 2 * ((j * 37) & 63) + flip)
            other = px * NGY + py
            pltpu.make_async_remote_copy(
                block(replies, other), block(returned, me), a2a_sem.at[4], a2a_sem.at[5],
                device_id=(px, py), device_id_type=MESH,
            ).start()
            return carry

        lax.fori_loop(1 - flip, NDEV // 2, send_back, 0)
    own_back = pltpu.make_async_copy(block(replies, me), block(returned, me), self_sem.at[2])
    own_back.start()

    solid_out[...] = done
    wait_sends(faces0)
    wait_sends(heat_copies)

    def sigma(x, carry):
        for j in range(2):
            y = WT - 1 + 2 * x + j
            s1[y, 8 : SR - 8, :] = lookup(mat[y, 8 : SR - 8, :], MODULUS) * s0[y, 8 : SR - 8, :]
        return carry

    lax.fori_loop(0, SX // 2 + 1, sigma, 0)
    lane = lax.broadcasted_iota(I32, (SY, LN), 1)

    def force(x, carry):
        c = s1[x + WT, R0 : R0 + SY, :]
        zp = jnp.where(lane == LN - 1, 0.0, pltpu.roll(c, LN - 1, 1))
        zm = jnp.where(lane == 0, 0.0, pltpu.roll(c, 1, 1))
        stress_out[0, x] = 0.5 * (
            s1[x + WT + 1, R0 : R0 + SY, :] - s1[x + WT - 1, R0 : R0 + SY, :]
        )
        stress_out[1, x] = 0.5 * (
            s1[x + WT, R0 + 1 : R0 + SY + 1, :] - s1[x + WT, R0 - 1 : R0 + SY - 1, :]
        )
        stress_out[2, x] = 0.5 * (zp - zm)
        return carry

    lax.fori_loop(0, SX, force, 0)

    wait_recvs(faces1)
    put_faces(f1, yrecv.at[1])

    def give(t, x, h, value):
        fluid_out[x, 16 * h : 16 * h + 16, t * LN : (t + 1) * LN] = value

    def step_two(x, carry):
        fluid_plane(f1, give, vel, flux, x)
        return carry

    lax.fori_loop(0, CX, step_two, 0)

    place.wait()
    own_back.wait()
    pltpu.make_async_copy(returned.at[pl.ds(0, count)], returned.at[pl.ds(0, count)], a2a_sem.at[5]).wait()

    def unpack(i, carry):
        for j in range(16):
            r = i * 16 + j
            wall_out[pl.ds(r, 1), :] = returned[pl.ds(dest_s[0, r], 1), :]
        return carry

    lax.fori_loop(0, ROWS // 16, unpack, 0)

    wait_sends(faces1)
    pltpu.make_async_copy(meta_out.at[pl.ds(0, NDEV - 1)], meta_out.at[pl.ds(0, NDEV - 1)], a2a_sem.at[0]).wait()
    pltpu.make_async_copy(outgoing.at[pl.ds(0, count)], outgoing.at[pl.ds(0, count)], a2a_sem.at[2]).wait()
    pltpu.make_async_copy(replies.at[pl.ds(0, count)], replies.at[pl.ds(0, count)], a2a_sem.at[4]).wait()


def store(*refs):
    sems = refs[-1]
    copies = [pltpu.make_async_copy(refs[i], refs[4 + i], sems.at[i]) for i in range(4)]
    for copy in copies:
        copy.start()
    for copy in copies:
        copy.wait()


def body(temp_fluid, velocity, wall_old, wall_mask, owner_map, slot_map, temp_solid, material):
    hbm_spec = pl.BlockSpec(memory_space=pltpu.HBM)
    vmem_spec = pl.BlockSpec(memory_space=pltpu.VMEM)
    vm = pltpu.VMEM
    padded = (NT, CX + 2, CY + 2 * PADY, LN)
    dma = pltpu.SemaphoreType.DMA
    fluid, wall, solid, stress = pl.pallas_call(
        kernel,
        out_shape=(
            jax.ShapeDtypeStruct((CX, CY, NT * LN), F32),
            jax.ShapeDtypeStruct((ROWS, LN), F32),
            jax.ShapeDtypeStruct((SX, SY, LN), F32),
            jax.ShapeDtypeStruct((3, SX, SY, LN), F32),
        ),
        in_specs=[hbm_spec] * 8,
        out_specs=(vmem_spec,) * 4,
        scratch_shapes=[
            vm(padded, F32), vm(padded, F32), vm((3, CX, CY, NT * LN), BF16),
            vm((CX, CY, LN), F32), vm((CX, CY, LN), I32), vm((ROWS, LN), F32),
            vm((1, ROWS), I32), vm((1, ROWS), I32), vm((1, ROWS), I32), pltpu.SMEM((1, ROWS), I32),
            vm((NDEV * CAP, LN), F32), vm((NDEV * CAP + CAP, LN), F32),
            vm((NDEV * CAP + CAP, LN), F32), vm((NDEV * CAP, LN), F32),
            vm((NDEV, 1, LN), F32), vm((NDEV, 1, LN), F32),
            vm((SP, SR, LN), F32), vm((SP, SR, LN), F32), vm((SP, SR, LN), I32),
            vm((SP, SR, LN), F32), vm((SP, SR, LN), F32),
            vm((2, 2, NT, CX, LN), F32), vm((2, 2, NT, CX, LN), F32),
            dma((16,)), dma((3,)), dma((10,)),
            dma((2, 4)), dma((2, 4)), dma((3, 8)), dma((3, 8)),
        ],
        compiler_params=pltpu.CompilerParams(
            collective_id=0, has_side_effects=True, vmem_limit_bytes=40 * 1024 * 1024
        ),
    )(*[
        pltpu.with_memory_space_constraint(x, pltpu.HBM)
        for x in (temp_fluid, velocity, wall_old, wall_mask,
        owner_map.reshape(1, ROWS), slot_map, temp_solid, material)
    ])
    results = (fluid, wall.reshape(CX, CY, LN), solid, stress)
    return pl.pallas_call(
        store,
        out_shape=tuple(jax.ShapeDtypeStruct(r.shape, F32) for r in results),
        in_specs=[pl.BlockSpec(memory_space=pl.ANY)] * 4,
        out_specs=(pl.BlockSpec(memory_space=pl.ANY),) * 4,
        scratch_shapes=[dma((4,))],
        compiler_params=pltpu.CompilerParams(vmem_limit_bytes=1024 * 1024),
    )(*results)


def solution(mesh):
    placed = (
        P("gx", "gy", None),
        P(None, "gx", "gy", None),
        P("gx", "gy", None),
        P("gx", "gy", None),
        P(("gx", "gy"), None, None),
        P(("gx", "gy"), None),
        P("gx", "gy", None),
        P("gx", "gy", None),
    )
    return jax.shard_map(
        body,
        mesh=mesh,
        in_specs=placed,
        out_specs=(
            P("gx", "gy", None),
            P("gx", "gy", None),
            P("gx", "gy", None),
            P(None, "gx", "gy", None),
        ),
        check_vma=False,
    )
```

```python
import functools

import jax
import jax.numpy as jnp
from jax import lax
from jax.experimental import pallas as pl
from jax.experimental.pallas import tpu as pltpu
from jax.sharding import PartitionSpec as P

MESH = pl.DeviceIdType.MESH
F32 = jnp.float32
BF16 = jnp.bfloat16
I32 = jnp.int32

NGX, NGY = 16, 8
NDEV = 128
CX, CY, NT, LN = 16, 64, 8, 128
SX, SY = 16, 32
CAP = 24
ROWS = 1024
SLOTS = 512
PADY = 8
WT = 5
WH = 4
SP = SX + 2 * WT
SR = 64
R0 = 16
CONDUCT = (0.05 * 0.4, 0.05 * 0.9, 0.05 * 1.5, 0.05 * 2.2)
MODULUS = (0.5, 1.0, 1.6, 2.4)
DIRS = [(dx, dy) for dx in (-1, 0, 1) for dy in (-1, 0, 1) if (dx, dy) != (0, 0)]


def peer_of(gx, gy, k):
    dc, dx, dy, dz = k & 1, (k >> 1) & 3, (k >> 3) & 3, (k >> 5) & 3
    c, z, x, y = gx & 1, gx >> 2, gy & 3, (gx & 2) | (gy >> 2)
    nc, nx, ny, nz = c ^ dc, (x + dx) & 3, (y + dy) & 3, (z + dz) & 3
    return (nz << 2) | (ny & 2) | nc, ((ny & 1) << 2) | nx


def halves(value):
    hi = value.astype(BF16)
    lo = (value - hi.astype(F32)).astype(BF16)
    return jnp.concatenate([hi, lo], axis=1)


def joined(product):
    return product[:, :LN] + product[:, LN:]


def onehot(mask):
    return jnp.where(mask, 1.0, 0.0).astype(BF16)


def lookup(material, table):
    out = jnp.where(material == 0, table[0], 0.0)
    for index in range(1, 4):
        out = jnp.where(material == index, table[index], out)
    return out.astype(F32)


def planes(step, width):
    if step > 0:
        return pl.ds(WT + SX - width, width), pl.ds(WT - width, width)
    if step < 0:
        return pl.ds(WT, width), pl.ds(WT + SX, width)
    return pl.ds(WT, SX), pl.ds(WT, SX)


def lines(step):
    if step > 0:
        return pl.ds(R0 + SY - 8, 8), pl.ds(R0 - 8, 8)
    if step < 0:
        return pl.ds(R0, 8), pl.ds(R0 + SY, 8)
    return pl.ds(R0, SY), pl.ds(R0, SY)


def inside(gx, gy, dx, dy):
    px, py = gx + dx, gy + dy
    return (px >= 0) & (px < NGX) & (py >= 0) & (py < NGY)


def spread_copies(ref, gx, gy, width, sends, recvs):
    out = []
    for i, (dx, dy) in enumerate(DIRS):
        xs, xd = planes(dx, width - 1 if dy else width)
        ys, yd = lines(dy)
        copy = pltpu.make_async_remote_copy(
            src_ref=ref.at[xs, ys, :],
            dst_ref=ref.at[xd, yd, :],
            send_sem=sends.at[i],
            recv_sem=recvs.at[i],
            device_id=(gx + dx, gy + dy),
            device_id_type=MESH,
        )
        out.append((copy, inside(gx, gy, dx, dy), inside(gx, gy, -dx, -dy)))
    return out


def start_all(copies):
    for copy, to, _ in copies:
        pl.when(to)(copy.start)


def wait_recvs(copies):
    for copy, _, came in copies:
        pl.when(came)(copy.wait_recv)


def wait_sends(copies):
    for copy, to, _ in copies:
        pl.when(to)(copy.wait_send)


def face_copies(field, ysend, yrecv, gx, gy, sends, recvs):
    out = []
    rows = pl.ds(PADY, CY)
    for i, step in enumerate((1, -1)):
        src, dst = (CX, 0) if step > 0 else (1, CX + 1)
        copy = pltpu.make_async_remote_copy(
            src_ref=field.at[:, src, rows, :],
            dst_ref=field.at[:, dst, rows, :],
            send_sem=sends.at[i],
            recv_sem=recvs.at[i],
            device_id=(gx + step, gy),
            device_id_type=MESH,
        )
        out.append((copy, inside(gx, gy, step, 0), inside(gx, gy, -step, 0)))
    for i, step in enumerate((1, -1)):
        copy = pltpu.make_async_remote_copy(
            src_ref=ysend.at[i],
            dst_ref=yrecv.at[i],
            send_sem=sends.at[2 + i],
            recv_sem=recvs.at[2 + i],
            device_id=(gx, gy + step),
            device_id_type=MESH,
        )
        out.append((copy, inside(gx, gy, 0, step), inside(gx, gy, 0, -step)))
    return out


def take_faces(field, ysend):
    for t in range(NT):
        ysend[0, t] = field[t, 1 : CX + 1, PADY + CY - 1, :]
        ysend[1, t] = field[t, 1 : CX + 1, PADY, :]


def put_faces(field, yrecv):
    for t in range(NT):
        field[t, 1 : CX + 1, PADY - 1, :] = yrecv[0, t]
        field[t, 1 : CX + 1, PADY + CY, :] = yrecv[1, t]


def fluid_plane(src, put, vel, flux, x):
    lane = lax.broadcasted_iota(I32, (16, LN), 1)
    first, last = lane == 0, lane == LN - 1
    zero = jnp.zeros((16, LN), F32)
    for h in range(CY // 16):
        r = PADY + 16 * h
        mids = [src[t, x + 1, r : r + 16, :] for t in range(NT)]
        ups = [pltpu.roll(c, LN - 1, 1) for c in mids] + [zero]
        downs = [zero] + [pltpu.roll(c, 1, 1) for c in mids]
        for t in range(NT):
            c = mids[t]
            pairs = (
                (src[t, x + 2, r : r + 16, :], src[t, x, r : r + 16, :]),
                (src[t, x + 1, r + 1 : r + 17, :], src[t, x + 1, r - 1 : r + 15, :]),
                (jnp.where(last, ups[t + 1], ups[t]), jnp.where(first, downs[t], downs[t + 1])),
            )
            total = None
            for k, (p, m) in enumerate(pairs):
                u = vel[k, x, 16 * h : 16 * h + 16, t * LN : (t + 1) * LN].astype(F32)
                a = jnp.maximum(u + 0.5, 0.5)
                pc = p - c
                term = a * ((m - c) + pc) - u * pc
                total = term if total is None else total + term
            if t == 0:
                total = total - flux[pl.ds(pl.multiple_of(x * CY + 16 * h, 16), 16), :]
            put(t, x, h, c + 0.1 * total)


def solid_step(src, dst, cond, heat, edge):
    lane = lax.broadcasted_iota(I32, (SR - 16, LN), 1)
    last, first = lane == LN - 1, lane == 0
    for x in range(edge, SP - edge):
        c = src[x, 8 : SR - 8, :]
        zp = jnp.where(last, 0.0, pltpu.roll(c, LN - 1, 1))
        zm = jnp.where(first, 0.0, pltpu.roll(c, 1, 1))
        beside = src[x + 1, 8 : SR - 8, :] + src[x - 1, 8 : SR - 8, :]
        beside = beside + (src[x, 9 : SR - 7, :] + src[x, 7 : SR - 9, :])
        lap = beside + (zp + zm) - 6.0 * c
        dst[x, 8 : SR - 8, :] = c + (cond[x, 8 : SR - 8, :] * lap + 0.2 * heat[x, 8 : SR - 8, :])


def kernel(
    fluid_in, vel_in, wall_in, mask_in, owner_in, slot_in, solid_in, mat_in,
    fluid_out, wall_out, solid_out, stress_out,
    f0, f1, vel, wall, mask, flux, owner, slot, dest, dest_s,
    outgoing, incoming, replies, returned, meta_out, meta_in,
    s0, s1, mat, cond, heat, ysend, yrecv,
    in_sem, self_sem, a2a_sem, fsend, frecv, ssend, srecv,
):
    gx, gy = lax.axis_index("gx"), lax.axis_index("gy")
    me = gx * NGY + gy

    loads = [
        pltpu.make_async_copy(owner_in, owner, in_sem.at[0]),
        pltpu.make_async_copy(slot_in, slot, in_sem.at[1]),
        pltpu.make_async_copy(wall_in, wall, in_sem.at[2]),
        pltpu.make_async_copy(mask_in, mask, in_sem.at[3]),
    ]
    interior = (pl.ds(1, CX), pl.ds(PADY, CY))
    tiles = [
        pltpu.make_async_copy(
            fluid_in.at[:, :, pl.ds(t * LN, LN)], f0.at[t, interior[0], interior[1], :], in_sem.at[4 + t]
        )
        for t in range(NT)
    ]
    core = (pl.ds(WT, SX), pl.ds(R0, SY))
    load_solid = pltpu.make_async_copy(solid_in, s0.at[core[0], core[1], :], in_sem.at[12])
    load_mat = pltpu.make_async_copy(mat_in, mat.at[core[0], core[1], :], in_sem.at[13])
    load_vel = pltpu.make_async_copy(vel_in, vel, in_sem.at[14])

    for ld in loads[:2]:
        ld.start()
    tiles[0].start()
    for ld in loads[2:]:
        ld.start()

    barrier = pltpu.get_barrier_semaphore()

    def greet(k, carry):
        px, py = peer_of(gx, gy, (k * 37) & 127)
        pl.semaphore_signal(barrier, inc=1, device_id=(px, py), device_id_type=MESH)
        return carry

    lax.fori_loop(1, NDEV, greet, 0)
    load_solid.start()
    load_mat.start()
    for t in range(1, NT):
        tiles[t].start()
    load_vel.start()


    def beyond(first, count, low, high):
        def clear(x, carry):
            for ref, value in ((s0, 0.0), (heat, 0.0), (mat, -1)):
                ref[first + x, low:high, :] = jnp.full((high - low, LN), value, ref.dtype)
            return carry

        lax.fori_loop(0, count, clear, 0)

    for side, at_edge in ((0, gx == 0), (1, gx == NGX - 1)):

        @pl.when(at_edge)
        def _(side=side):
            for field in (f0, f1):
                for t in range(NT):
                    field[t, side * (CX + 1)] = jnp.zeros((CY + 2 * PADY, LN), F32)
            beyond(side * (WT + SX), WT, 8, SR - 8)

    for side, at_edge in ((0, gy == 0), (1, gy == NGY - 1)):

        @pl.when(at_edge)
        def _(side=side):
            for turn in range(2):
                yrecv[turn, side] = jnp.zeros((NT, CX, LN), F32)
            low = R0 - 8 + side * (SY + 8)
            beyond(0, SP, low, low + 8)

    loads[0].wait()
    loads[1].wait()
    own_row = owner[...]
    mine = own_row == lax.broadcasted_iota(I32, (NDEV, ROWS), 0)
    mine_b = onehot(mine)
    before = onehot(
        lax.broadcasted_iota(I32, (ROWS, ROWS), 0) < lax.broadcasted_iota(I32, (ROWS, ROWS), 1)
    )
    ranks = jnp.dot(mine_b, before, preferred_element_type=F32)
    rank_row = jnp.sum(jnp.where(mine, ranks, 0.0), axis=0, keepdims=True).astype(I32)
    dest[...] = jnp.clip(own_row * CAP + rank_row, 0, NDEV * CAP - 1)
    place = pltpu.make_async_copy(dest, dest_s, in_sem.at[15])
    place.start()
    code = slot[...] + 1
    at_rank = onehot(rank_row == lax.broadcasted_iota(I32, (LN, ROWS), 0))
    parts = []
    for part in (code & 15, code >> 4):
        left = jnp.where(mine, part.astype(F32), 0.0).astype(BF16)
        parts.append(
            lax.dot_general(left, at_rank, (((1,), (1,)), ((), ())), preferred_element_type=F32)
        )
    meta_out[...] = (parts[0] + 16.0 * parts[1]).reshape(NDEV, 1, LN)

    for ld in loads[2:]:
        ld.wait()
    tiles[0].wait()
    for x in range(CX):
        t0 = f0[0, x + 1, PADY : PADY + CY, :]
        flux[x * CY : (x + 1) * CY, :] = mask[x].astype(F32) * 2.0 * (t0 - wall[x])
    flux_b = halves(flux[...])
    chunk = 16 * CAP

    def pack(i, carry):
        base = pl.multiple_of(i * chunk, chunk)
        pick = onehot(dest[...] == lax.broadcasted_iota(I32, (chunk, ROWS), 0) + base)
        outgoing[pl.ds(base, chunk), :] = joined(jnp.dot(pick, flux_b, preferred_element_type=F32))
        return carry

    lax.fori_loop(0, NDEV // 16, pack, 0)

    for t in range(1, NT):
        tiles[t].wait()
    take_faces(f0, ysend.at[0])
    faces0 = face_copies(f0, ysend.at[0], yrecv.at[0], gx, gy, fsend.at[0], frecv.at[0])
    pl.semaphore_wait(barrier, NDEV - 1)

    def block(ref, d):
        return ref.at[pl.ds(pl.multiple_of(d * CAP, CAP), CAP), :]

    def send_rows(k, carry):
        px, py = peer_of(gx, gy, (k * 37) & 127)
        other = px * NGY + py
        pltpu.make_async_remote_copy(
            meta_out.at[other], meta_in.at[me], a2a_sem.at[0], a2a_sem.at[1],
            device_id=(px, py), device_id_type=MESH,
        ).start()
        pltpu.make_async_remote_copy(
            block(outgoing, other), block(incoming, me), a2a_sem.at[2], a2a_sem.at[3],
            device_id=(px, py), device_id_type=MESH,
        ).start()
        return carry

    lax.fori_loop(1, 40, send_rows, 0)
    start_all(faces0)
    lax.fori_loop(40, NDEV, send_rows, 0)
    own_meta = pltpu.make_async_copy(meta_out.at[me], meta_in.at[me], self_sem.at[0])
    own_rows = pltpu.make_async_copy(block(outgoing, me), block(incoming, me), self_sem.at[1])
    own_meta.start()
    own_rows.start()

    load_solid.wait()
    load_mat.wait()
    temp_copies = spread_copies(s0, gx, gy, WT, ssend.at[0], srecv.at[0])
    mat_copies = spread_copies(mat, gx, gy, WH, ssend.at[1], srecv.at[1])
    start_all(temp_copies)
    start_all(mat_copies)

    load_vel.wait()
    wait_recvs(faces0)
    put_faces(f0, yrecv.at[0])

    def keep(t, x, h, value):
        f1[t, x + 1, PADY + 16 * h : PADY + 16 * h + 16, :] = value

    def step_one(x, carry):
        fluid_plane(f0, keep, vel, flux, x)
        return carry

    lax.fori_loop(0, CX, step_one, 0)

    take_faces(f1, ysend.at[1])
    faces1 = face_copies(f1, ysend.at[1], yrecv.at[1], gx, gy, fsend.at[1], frecv.at[1])

    count = (NDEV - 1) * CAP
    own_meta.wait()
    own_rows.wait()
    pltpu.make_async_copy(meta_in.at[pl.ds(0, NDEV - 1)], meta_in.at[pl.ds(0, NDEV - 1)], a2a_sem.at[1]).wait()
    pltpu.make_async_copy(incoming.at[pl.ds(0, count)], incoming.at[pl.ds(0, count)], a2a_sem.at[3]).wait()
    slots_in = meta_in[...].reshape(NDEV, LN)
    slots_t = slots_in.T
    wanted = lax.broadcasted_iota(I32, (SLOTS, NDEV), 0).astype(F32) + 1.0
    total = None
    for first in range(0, CAP, 6):
        span = range(first, first + 6)
        hits = jnp.concatenate([onehot(slots_t[k : k + 1, :] == wanted) for k in span], axis=1)
        rows = jnp.concatenate(
            [halves(incoming[pl.ds(k, NDEV, stride=CAP), :]) for k in span], axis=0
        )
        some = jnp.dot(hits, rows, preferred_element_type=F32)
        total = some if total is None else total + some
    heat[WT : WT + SX, R0 : R0 + SY, :] = joined(total).reshape(SX, SY, LN)
    heat_copies = spread_copies(heat, gx, gy, WH, ssend.at[2], srecv.at[2])
    start_all(heat_copies)
    start_all(faces1)
    wait_recvs(temp_copies)
    wait_recvs(mat_copies)

    def conduct(x, carry):
        for j in range(2):
            cond[2 * x + j, 8 : SR - 8, :] = lookup(mat[2 * x + j, 8 : SR - 8, :], CONDUCT)
        return carry

    lax.fori_loop(0, SP // 2, conduct, 0)

    wait_sends(temp_copies)
    wait_sends(mat_copies)
    wait_recvs(heat_copies)

    solid_step(s0, s1, cond, heat, 1)
    solid_step(s1, s0, cond, heat, 2)
    solid_step(s0, s1, cond, heat, 3)
    solid_step(s1, s0, cond, heat, 4)

    done = s0[WT : WT + SX, R0 : R0 + SY, :]
    done_b = halves(done.reshape(SLOTS, LN))
    column = lax.broadcasted_iota(I32, (NDEV // 2, SLOTS), 1).astype(F32) + 1.0
    for core in range(2):
        starts = [(2 * g + core) * NGY for g in range(NGX // 2)]
        some_slots = jnp.concatenate(
            [meta_in[b : b + NGY].reshape(NGY, LN) for b in starts], axis=0
        )
        hits = jnp.concatenate(
            [onehot(some_slots[:, k : k + 1] == column) for k in range(CAP)], axis=0
        )
        picked = joined(jnp.dot(hits, done_b, preferred_element_type=F32))
        for k in range(CAP):
            for g, b in enumerate(starts):
                r = k * (NDEV // 2) + g * NGY
                replies[pl.ds(b * CAP + k, NGY, stride=CAP), :] = picked[r : r + NGY]
        flip = (gx & 1) ^ core

        def send_back(j, carry):
            px, py = peer_of(gx, gy, 2 * ((j * 37) & 63) + flip)
            other = px * NGY + py
            pltpu.make_async_remote_copy(
                block(replies, other), block(returned, me), a2a_sem.at[4], a2a_sem.at[5],
                device_id=(px, py), device_id_type=MESH,
            ).start()
            return carry

        lax.fori_loop(1 - flip, NDEV // 2, send_back, 0)
    own_back = pltpu.make_async_copy(block(replies, me), block(returned, me), self_sem.at[2])
    own_back.start()

    solid_out[...] = done
    wait_sends(faces0)
    wait_sends(heat_copies)

    def sigma(x, carry):
        for j in range(2):
            y = WT - 1 + 2 * x + j
            s1[y, 8 : SR - 8, :] = lookup(mat[y, 8 : SR - 8, :], MODULUS) * s0[y, 8 : SR - 8, :]
        return carry

    lax.fori_loop(0, SX // 2 + 1, sigma, 0)
    lane = lax.broadcasted_iota(I32, (SY, LN), 1)

    def force(x, carry):
        c = s1[x + WT, R0 : R0 + SY, :]
        zp = jnp.where(lane == LN - 1, 0.0, pltpu.roll(c, LN - 1, 1))
        zm = jnp.where(lane == 0, 0.0, pltpu.roll(c, 1, 1))
        stress_out[0, x] = 0.5 * (
            s1[x + WT + 1, R0 : R0 + SY, :] - s1[x + WT - 1, R0 : R0 + SY, :]
        )
        stress_out[1, x] = 0.5 * (
            s1[x + WT, R0 + 1 : R0 + SY + 1, :] - s1[x + WT, R0 - 1 : R0 + SY - 1, :]
        )
        stress_out[2, x] = 0.5 * (zp - zm)
        return carry

    lax.fori_loop(0, SX, force, 0)

    wait_recvs(faces1)
    put_faces(f1, yrecv.at[1])

    def give(t, x, h, value):
        fluid_out[x, 16 * h : 16 * h + 16, t * LN : (t + 1) * LN] = value

    def step_two(x, carry):
        fluid_plane(f1, give, vel, flux, x)
        return carry

    lax.fori_loop(0, CX, step_two, 0)

    place.wait()
    own_back.wait()
    pltpu.make_async_copy(returned.at[pl.ds(0, count)], returned.at[pl.ds(0, count)], a2a_sem.at[5]).wait()

    def unpack(i, carry):
        for j in range(16):
            r = i * 16 + j
            wall_out[pl.ds(r, 1), :] = returned[pl.ds(dest_s[0, r], 1), :]
        return carry

    lax.fori_loop(0, ROWS // 16, unpack, 0)

    wait_sends(faces1)
    pltpu.make_async_copy(meta_out.at[pl.ds(0, NDEV - 1)], meta_out.at[pl.ds(0, NDEV - 1)], a2a_sem.at[0]).wait()
    pltpu.make_async_copy(outgoing.at[pl.ds(0, count)], outgoing.at[pl.ds(0, count)], a2a_sem.at[2]).wait()
    pltpu.make_async_copy(replies.at[pl.ds(0, count)], replies.at[pl.ds(0, count)], a2a_sem.at[4]).wait()


def store(*refs):
    sems = refs[-1]
    pieces = CX // 2
    copies = [
        pltpu.make_async_copy(
            refs[0].at[pl.ds(2 * i, 2)], refs[4].at[pl.ds(2 * i, 2)], sems.at[i]
        )
        for i in range(pieces)
    ]
    copies += [
        pltpu.make_async_copy(refs[i], refs[4 + i], sems.at[pieces + i]) for i in range(1, 4)
    ]
    for copy in copies:
        copy.start()
    for copy in copies:
        copy.wait()


def body(temp_fluid, velocity, wall_old, wall_mask, owner_map, slot_map, temp_solid, material):
    hbm_spec = pl.BlockSpec(memory_space=pltpu.HBM)
    vmem_spec = pl.BlockSpec(memory_space=pltpu.VMEM)
    vm = pltpu.VMEM
    padded = (NT, CX + 2, CY + 2 * PADY, LN)
    dma = pltpu.SemaphoreType.DMA
    fluid, wall, solid, stress = pl.pallas_call(
        kernel,
        out_shape=(
            jax.ShapeDtypeStruct((CX, CY, NT * LN), F32),
            jax.ShapeDtypeStruct((ROWS, LN), F32),
            jax.ShapeDtypeStruct((SX, SY, LN), F32),
            jax.ShapeDtypeStruct((3, SX, SY, LN), F32),
        ),
        in_specs=[hbm_spec] * 8,
        out_specs=(vmem_spec,) * 4,
        scratch_shapes=[
            vm(padded, F32), vm(padded, F32), vm((3, CX, CY, NT * LN), BF16),
            vm((CX, CY, LN), F32), vm((CX, CY, LN), I32), vm((ROWS, LN), F32),
            vm((1, ROWS), I32), vm((1, ROWS), I32), vm((1, ROWS), I32), pltpu.SMEM((1, ROWS), I32),
            vm((NDEV * CAP, LN), F32), vm((NDEV * CAP + CAP, LN), F32),
            vm((NDEV * CAP + CAP, LN), F32), vm((NDEV * CAP, LN), F32),
            vm((NDEV, 1, LN), F32), vm((NDEV, 1, LN), F32),
            vm((SP, SR, LN), F32), vm((SP, SR, LN), F32), vm((SP, SR, LN), I32),
            vm((SP, SR, LN), F32), vm((SP, SR, LN), F32),
            vm((2, 2, NT, CX, LN), F32), vm((2, 2, NT, CX, LN), F32),
            dma((16,)), dma((3,)), dma((10,)),
            dma((2, 4)), dma((2, 4)), dma((3, 8)), dma((3, 8)),
        ],
        compiler_params=pltpu.CompilerParams(
            collective_id=0, has_side_effects=True, vmem_limit_bytes=40 * 1024 * 1024
        ),
    )(*[
        pltpu.with_memory_space_constraint(x, pltpu.HBM)
        for x in (temp_fluid, velocity, wall_old, wall_mask,
        owner_map.reshape(1, ROWS), slot_map, temp_solid, material)
    ])
    results = (fluid, wall.reshape(CX, CY, LN), solid, stress)
    return pl.pallas_call(
        store,
        out_shape=tuple(jax.ShapeDtypeStruct(r.shape, F32) for r in results),
        in_specs=[pl.BlockSpec(memory_space=pl.ANY)] * 4,
        out_specs=(pl.BlockSpec(memory_space=pl.ANY),) * 4,
        scratch_shapes=[dma((CX // 2 + 4,))],
        compiler_params=pltpu.CompilerParams(vmem_limit_bytes=1024 * 1024),
    )(*results)


def solution(mesh):
    placed = (
        P("gx", "gy", None),
        P(None, "gx", "gy", None),
        P("gx", "gy", None),
        P("gx", "gy", None),
        P(("gx", "gy"), None, None),
        P(("gx", "gy"), None),
        P("gx", "gy", None),
        P("gx", "gy", None),
    )
    return jax.shard_map(
        body,
        mesh=mesh,
        in_specs=placed,
        out_specs=(
            P("gx", "gy", None),
            P("gx", "gy", None),
            P("gx", "gy", None),
            P(None, "gx", "gy", None),
        ),
        check_vma=False,
    )
```

```python
import functools

import jax
import jax.numpy as jnp
from jax import lax
from jax.experimental import pallas as pl
from jax.experimental.pallas import tpu as pltpu
from jax.sharding import PartitionSpec as P

MESH = pl.DeviceIdType.MESH
F32 = jnp.float32
BF16 = jnp.bfloat16
I32 = jnp.int32

NGX, NGY = 16, 8
NDEV = 128
CX, CY, NT, LN = 16, 64, 8, 128
SX, SY = 16, 32
CAP = 24
ROWS = 1024
SLOTS = 512
PADY = 8
WT = 5
WH = 4
SP = SX + 2 * WT
SR = 64
R0 = 16
CONDUCT = (0.05 * 0.4, 0.05 * 0.9, 0.05 * 1.5, 0.05 * 2.2)
MODULUS = (0.5, 1.0, 1.6, 2.4)
DIRS = [(dx, dy) for dx in (-1, 0, 1) for dy in (-1, 0, 1) if (dx, dy) != (0, 0)]


def peer_of(gx, gy, k):
    dc, dx, dy, dz = k & 1, (k >> 1) & 3, (k >> 3) & 3, (k >> 5) & 3
    c, z, x, y = gx & 1, gx >> 2, gy & 3, (gx & 2) | (gy >> 2)
    nc, nx, ny, nz = c ^ dc, (x + dx) & 3, (y + dy) & 3, (z + dz) & 3
    return (nz << 2) | (ny & 2) | nc, ((ny & 1) << 2) | nx


def halves(value):
    hi = value.astype(BF16)
    lo = (value - hi.astype(F32)).astype(BF16)
    return jnp.concatenate([hi, lo], axis=1)


def joined(product):
    return product[:, :LN] + product[:, LN:]


def onehot(mask):
    return jnp.where(mask, 1.0, 0.0).astype(BF16)


def lookup(material, table):
    out = jnp.where(material == 0, table[0], 0.0)
    for index in range(1, 4):
        out = jnp.where(material == index, table[index], out)
    return out.astype(F32)


def planes(step, width):
    if step > 0:
        return pl.ds(WT + SX - width, width), pl.ds(WT - width, width)
    if step < 0:
        return pl.ds(WT, width), pl.ds(WT + SX, width)
    return pl.ds(WT, SX), pl.ds(WT, SX)


def lines(step):
    if step > 0:
        return pl.ds(R0 + SY - 8, 8), pl.ds(R0 - 8, 8)
    if step < 0:
        return pl.ds(R0, 8), pl.ds(R0 + SY, 8)
    return pl.ds(R0, SY), pl.ds(R0, SY)


def inside(gx, gy, dx, dy):
    px, py = gx + dx, gy + dy
    return (px >= 0) & (px < NGX) & (py >= 0) & (py < NGY)


def spread_copies(ref, gx, gy, width, sends, recvs):
    out = []
    for i, (dx, dy) in enumerate(DIRS):
        xs, xd = planes(dx, width - 1 if dy else width)
        ys, yd = lines(dy)
        copy = pltpu.make_async_remote_copy(
            src_ref=ref.at[xs, ys, :],
            dst_ref=ref.at[xd, yd, :],
            send_sem=sends.at[i],
            recv_sem=recvs.at[i],
            device_id=(gx + dx, gy + dy),
            device_id_type=MESH,
        )
        out.append((copy, inside(gx, gy, dx, dy), inside(gx, gy, -dx, -dy)))
    return out


def start_all(copies):
    for copy, to, _ in copies:
        pl.when(to)(copy.start)


def wait_recvs(copies):
    for copy, _, came in copies:
        pl.when(came)(copy.wait_recv)


def wait_sends(copies):
    for copy, to, _ in copies:
        pl.when(to)(copy.wait_send)


def face_copies(field, ysend, yrecv, gx, gy, sends, recvs):
    out = []
    rows = pl.ds(PADY, CY)
    for i, step in enumerate((1, -1)):
        src, dst = (CX, 0) if step > 0 else (1, CX + 1)
        copy = pltpu.make_async_remote_copy(
            src_ref=field.at[:, src, rows, :],
            dst_ref=field.at[:, dst, rows, :],
            send_sem=sends.at[i],
            recv_sem=recvs.at[i],
            device_id=(gx + step, gy),
            device_id_type=MESH,
        )
        out.append((copy, inside(gx, gy, step, 0), inside(gx, gy, -step, 0)))
    for i, step in enumerate((1, -1)):
        copy = pltpu.make_async_remote_copy(
            src_ref=ysend.at[i],
            dst_ref=yrecv.at[i],
            send_sem=sends.at[2 + i],
            recv_sem=recvs.at[2 + i],
            device_id=(gx, gy + step),
            device_id_type=MESH,
        )
        out.append((copy, inside(gx, gy, 0, step), inside(gx, gy, 0, -step)))
    return out


def take_faces(field, ysend):
    for t in range(NT):
        ysend[0, t] = field[t, 1 : CX + 1, PADY + CY - 1, :]
        ysend[1, t] = field[t, 1 : CX + 1, PADY, :]


def put_faces(field, yrecv):
    for t in range(NT):
        field[t, 1 : CX + 1, PADY - 1, :] = yrecv[0, t]
        field[t, 1 : CX + 1, PADY + CY, :] = yrecv[1, t]


def fluid_plane(src, put, vel, flux, x):
    lane = lax.broadcasted_iota(I32, (16, LN), 1)
    first, last = lane == 0, lane == LN - 1
    zero = jnp.zeros((16, LN), F32)
    for h in range(CY // 16):
        r = PADY + 16 * h
        mids = [src[t, x + 1, r : r + 16, :] for t in range(NT)]
        ups = [pltpu.roll(c, LN - 1, 1) for c in mids] + [zero]
        downs = [zero] + [pltpu.roll(c, 1, 1) for c in mids]
        for t in range(NT):
            c = mids[t]
            pairs = (
                (src[t, x + 2, r : r + 16, :], src[t, x, r : r + 16, :]),
                (src[t, x + 1, r + 1 : r + 17, :], src[t, x + 1, r - 1 : r + 15, :]),
                (jnp.where(last, ups[t + 1], ups[t]), jnp.where(first, downs[t], downs[t + 1])),
            )
            total = None
            for k, (p, m) in enumerate(pairs):
                u = vel[k, x, 16 * h : 16 * h + 16, t * LN : (t + 1) * LN].astype(F32)
                a = jnp.maximum(u + 0.5, 0.5)
                pc = p - c
                term = a * ((m - c) + pc) - u * pc
                total = term if total is None else total + term
            if t == 0:
                total = total - flux[pl.ds(pl.multiple_of(x * CY + 16 * h, 16), 16), :]
            put(t, x, h, c + 0.1 * total)


def solid_step(src, dst, cond, heat, edge):
    lane = lax.broadcasted_iota(I32, (SR - 16, LN), 1)
    last, first = lane == LN - 1, lane == 0
    for x in range(edge, SP - edge):
        c = src[x, 8 : SR - 8, :]
        zp = jnp.where(last, 0.0, pltpu.roll(c, LN - 1, 1))
        zm = jnp.where(first, 0.0, pltpu.roll(c, 1, 1))
        beside = src[x + 1, 8 : SR - 8, :] + src[x - 1, 8 : SR - 8, :]
        beside = beside + (src[x, 9 : SR - 7, :] + src[x, 7 : SR - 9, :])
        lap = beside + (zp + zm) - 6.0 * c
        dst[x, 8 : SR - 8, :] = c + (cond[x, 8 : SR - 8, :] * lap + 0.2 * heat[x, 8 : SR - 8, :])


def kernel(
    fluid_in, vel_in, wall_in, mask_in, owner_in, slot_in, solid_in, mat_in,
    fluid_out, wall_out, solid_out, stress_out,
    f0, f1, vel, wall, mask, flux, owner, slot, dest, dest_s,
    outgoing, incoming, replies, returned, meta_out, meta_in,
    s0, s1, mat, cond, heat, ysend, yrecv,
    in_sem, self_sem, a2a_sem, fsend, frecv, ssend, srecv,
):
    gx, gy = lax.axis_index("gx"), lax.axis_index("gy")
    me = gx * NGY + gy

    loads = [
        pltpu.make_async_copy(owner_in, owner, in_sem.at[0]),
        pltpu.make_async_copy(slot_in, slot, in_sem.at[1]),
        pltpu.make_async_copy(wall_in, wall, in_sem.at[2]),
        pltpu.make_async_copy(mask_in, mask, in_sem.at[3]),
    ]
    interior = (pl.ds(1, CX), pl.ds(PADY, CY))
    tiles = [
        pltpu.make_async_copy(
            fluid_in.at[:, :, pl.ds(t * LN, LN)], f0.at[t, interior[0], interior[1], :], in_sem.at[4 + t]
        )
        for t in range(NT)
    ]
    core = (pl.ds(WT, SX), pl.ds(R0, SY))
    load_solid = pltpu.make_async_copy(solid_in, s0.at[core[0], core[1], :], in_sem.at[12])
    load_mat = pltpu.make_async_copy(mat_in, mat.at[core[0], core[1], :], in_sem.at[13])
    load_vel = pltpu.make_async_copy(vel_in, vel, in_sem.at[14])

    for ld in loads[:2]:
        ld.start()
    tiles[0].start()
    for ld in loads[2:]:
        ld.start()

    barrier = pltpu.get_barrier_semaphore()

    def greet(k, carry):
        px, py = peer_of(gx, gy, (k * 37) & 127)
        pl.semaphore_signal(barrier, inc=1, device_id=(px, py), device_id_type=MESH)
        return carry

    lax.fori_loop(1, NDEV, greet, 0)
    load_solid.start()
    load_mat.start()
    for t in range(1, NT):
        tiles[t].start()
    load_vel.start()


    def beyond(first, count, low, high):
        def clear(x, carry):
            for ref, value in ((s0, 0.0), (heat, 0.0), (mat, -1)):
                ref[first + x, low:high, :] = jnp.full((high - low, LN), value, ref.dtype)
            return carry

        lax.fori_loop(0, count, clear, 0)

    for side, at_edge in ((0, gx == 0), (1, gx == NGX - 1)):

        @pl.when(at_edge)
        def _(side=side):
            for field in (f0, f1):
                for t in range(NT):
                    field[t, side * (CX + 1)] = jnp.zeros((CY + 2 * PADY, LN), F32)
            beyond(side * (WT + SX), WT, 8, SR - 8)

    for side, at_edge in ((0, gy == 0), (1, gy == NGY - 1)):

        @pl.when(at_edge)
        def _(side=side):
            for turn in range(2):
                yrecv[turn, side] = jnp.zeros((NT, CX, LN), F32)
            low = R0 - 8 + side * (SY + 8)
            beyond(0, SP, low, low + 8)

    loads[0].wait()
    loads[1].wait()
    own_row = owner[...]
    mine = own_row == lax.broadcasted_iota(I32, (NDEV, ROWS), 0)
    mine_b = onehot(mine)
    before = onehot(
        lax.broadcasted_iota(I32, (ROWS, ROWS), 0) < lax.broadcasted_iota(I32, (ROWS, ROWS), 1)
    )
    ranks = jnp.dot(mine_b, before, preferred_element_type=F32)
    rank_row = jnp.sum(jnp.where(mine, ranks, 0.0), axis=0, keepdims=True).astype(I32)
    dest[...] = jnp.clip(own_row * CAP + rank_row, 0, NDEV * CAP - 1)
    place = pltpu.make_async_copy(dest, dest_s, in_sem.at[15])
    place.start()
    code = slot[...] + 1
    at_rank = onehot(rank_row == lax.broadcasted_iota(I32, (LN, ROWS), 0))
    parts = []
    for part in (code & 15, code >> 4):
        left = jnp.where(mine, part.astype(F32), 0.0).astype(BF16)
        parts.append(
            lax.dot_general(left, at_rank, (((1,), (1,)), ((), ())), preferred_element_type=F32)
        )
    meta_out[...] = (parts[0] + 16.0 * parts[1]).reshape(NDEV, 1, LN)

    for ld in loads[2:]:
        ld.wait()
    tiles[0].wait()
    for x in range(CX):
        t0 = f0[0, x + 1, PADY : PADY + CY, :]
        flux[x * CY : (x + 1) * CY, :] = mask[x].astype(F32) * 2.0 * (t0 - wall[x])
    flux_b = halves(flux[...])
    chunk = 16 * CAP

    def pack(i, carry):
        base = pl.multiple_of(i * chunk, chunk)
        pick = onehot(dest[...] == lax.broadcasted_iota(I32, (chunk, ROWS), 0) + base)
        outgoing[pl.ds(base, chunk), :] = joined(jnp.dot(pick, flux_b, preferred_element_type=F32))
        return carry

    lax.fori_loop(0, NDEV // 16, pack, 0)

    for t in range(1, NT):
        tiles[t].wait()
    take_faces(f0, ysend.at[0])
    faces0 = face_copies(f0, ysend.at[0], yrecv.at[0], gx, gy, fsend.at[0], frecv.at[0])
    pl.semaphore_wait(barrier, NDEV - 1)

    def block(ref, d):
        return ref.at[pl.ds(pl.multiple_of(d * CAP, CAP), CAP), :]

    def send_rows(k, carry):
        px, py = peer_of(gx, gy, (k * 37) & 127)
        other = px * NGY + py
        pltpu.make_async_remote_copy(
            meta_out.at[other], meta_in.at[me], a2a_sem.at[0], a2a_sem.at[1],
            device_id=(px, py), device_id_type=MESH,
        ).start()
        pltpu.make_async_remote_copy(
            block(outgoing, other), block(incoming, me), a2a_sem.at[2], a2a_sem.at[3],
            device_id=(px, py), device_id_type=MESH,
        ).start()
        return carry

    lax.fori_loop(1, 40, send_rows, 0)
    start_all(faces0)
    lax.fori_loop(40, NDEV, send_rows, 0)
    own_meta = pltpu.make_async_copy(meta_out.at[me], meta_in.at[me], self_sem.at[0])
    own_rows = pltpu.make_async_copy(block(outgoing, me), block(incoming, me), self_sem.at[1])
    own_meta.start()
    own_rows.start()

    load_vel.wait()
    wait_recvs(faces0)
    put_faces(f0, yrecv.at[0])

    def keep(t, x, h, value):
        f1[t, x + 1, PADY + 16 * h : PADY + 16 * h + 16, :] = value

    def step_one(x, carry):
        fluid_plane(f0, keep, vel, flux, x)
        return carry

    lax.fori_loop(0, CX, step_one, 0)

    load_solid.wait()
    load_mat.wait()
    temp_copies = spread_copies(s0, gx, gy, WT, ssend.at[0], srecv.at[0])
    mat_copies = spread_copies(mat, gx, gy, WH, ssend.at[1], srecv.at[1])
    start_all(temp_copies)
    start_all(mat_copies)

    take_faces(f1, ysend.at[1])
    faces1 = face_copies(f1, ysend.at[1], yrecv.at[1], gx, gy, fsend.at[1], frecv.at[1])

    count = (NDEV - 1) * CAP
    own_meta.wait()
    own_rows.wait()
    pltpu.make_async_copy(meta_in.at[pl.ds(0, NDEV - 1)], meta_in.at[pl.ds(0, NDEV - 1)], a2a_sem.at[1]).wait()
    pltpu.make_async_copy(incoming.at[pl.ds(0, count)], incoming.at[pl.ds(0, count)], a2a_sem.at[3]).wait()
    slots_in = meta_in[...].reshape(NDEV, LN)
    slots_t = slots_in.T
    wanted = lax.broadcasted_iota(I32, (SLOTS, NDEV), 0).astype(F32) + 1.0
    total = None
    for first in range(0, CAP, 6):
        span = range(first, first + 6)
        hits = jnp.concatenate([onehot(slots_t[k : k + 1, :] == wanted) for k in span], axis=1)
        rows = jnp.concatenate(
            [halves(incoming[pl.ds(k, NDEV, stride=CAP), :]) for k in span], axis=0
        )
        some = jnp.dot(hits, rows, preferred_element_type=F32)
        total = some if total is None else total + some
    heat[WT : WT + SX, R0 : R0 + SY, :] = joined(total).reshape(SX, SY, LN)
    heat_copies = spread_copies(heat, gx, gy, WH, ssend.at[2], srecv.at[2])
    start_all(heat_copies)
    start_all(faces1)
    wait_recvs(temp_copies)
    wait_recvs(mat_copies)

    def conduct(x, carry):
        for j in range(2):
            cond[2 * x + j, 8 : SR - 8, :] = lookup(mat[2 * x + j, 8 : SR - 8, :], CONDUCT)
        return carry

    lax.fori_loop(0, SP // 2, conduct, 0)

    wait_sends(temp_copies)
    wait_sends(mat_copies)
    wait_recvs(heat_copies)

    solid_step(s0, s1, cond, heat, 1)
    solid_step(s1, s0, cond, heat, 2)
    solid_step(s0, s1, cond, heat, 3)
    solid_step(s1, s0, cond, heat, 4)

    done = s0[WT : WT + SX, R0 : R0 + SY, :]
    done_b = halves(done.reshape(SLOTS, LN))
    column = lax.broadcasted_iota(I32, (NDEV // 2, SLOTS), 1).astype(F32) + 1.0
    for core in range(2):
        starts = [(2 * g + core) * NGY for g in range(NGX // 2)]
        some_slots = jnp.concatenate(
            [meta_in[b : b + NGY].reshape(NGY, LN) for b in starts], axis=0
        )
        hits = jnp.concatenate(
            [onehot(some_slots[:, k : k + 1] == column) for k in range(CAP)], axis=0
        )
        picked = joined(jnp.dot(hits, done_b, preferred_element_type=F32))
        for k in range(CAP):
            for g, b in enumerate(starts):
                r = k * (NDEV // 2) + g * NGY
                replies[pl.ds(b * CAP + k, NGY, stride=CAP), :] = picked[r : r + NGY]
        flip = (gx & 1) ^ core

        def send_back(j, carry):
            px, py = peer_of(gx, gy, 2 * ((j * 37) & 63) + flip)
            other = px * NGY + py
            pltpu.make_async_remote_copy(
                block(replies, other), block(returned, me), a2a_sem.at[4], a2a_sem.at[5],
                device_id=(px, py), device_id_type=MESH,
            ).start()
            return carry

        lax.fori_loop(1 - flip, NDEV // 2, send_back, 0)
    own_back = pltpu.make_async_copy(block(replies, me), block(returned, me), self_sem.at[2])
    own_back.start()

    solid_out[...] = done
    wait_sends(faces0)
    wait_sends(heat_copies)

    def sigma(x, carry):
        for j in range(2):
            y = WT - 1 + 2 * x + j
            s1[y, 8 : SR - 8, :] = lookup(mat[y, 8 : SR - 8, :], MODULUS) * s0[y, 8 : SR - 8, :]
        return carry

    lax.fori_loop(0, SX // 2 + 1, sigma, 0)
    lane = lax.broadcasted_iota(I32, (SY, LN), 1)

    def force(x, carry):
        c = s1[x + WT, R0 : R0 + SY, :]
        zp = jnp.where(lane == LN - 1, 0.0, pltpu.roll(c, LN - 1, 1))
        zm = jnp.where(lane == 0, 0.0, pltpu.roll(c, 1, 1))
        stress_out[0, x] = 0.5 * (
            s1[x + WT + 1, R0 : R0 + SY, :] - s1[x + WT - 1, R0 : R0 + SY, :]
        )
        stress_out[1, x] = 0.5 * (
            s1[x + WT, R0 + 1 : R0 + SY + 1, :] - s1[x + WT, R0 - 1 : R0 + SY - 1, :]
        )
        stress_out[2, x] = 0.5 * (zp - zm)
        return carry

    lax.fori_loop(0, SX, force, 0)

    wait_recvs(faces1)
    put_faces(f1, yrecv.at[1])

    def give(t, x, h, value):
        fluid_out[x, 16 * h : 16 * h + 16, t * LN : (t + 1) * LN] = value

    def step_two(x, carry):
        fluid_plane(f1, give, vel, flux, x)
        return carry

    lax.fori_loop(0, CX, step_two, 0)

    place.wait()
    own_back.wait()
    pltpu.make_async_copy(returned.at[pl.ds(0, count)], returned.at[pl.ds(0, count)], a2a_sem.at[5]).wait()

    def unpack(i, carry):
        for j in range(16):
            r = i * 16 + j
            wall_out[pl.ds(r, 1), :] = returned[pl.ds(dest_s[0, r], 1), :]
        return carry

    lax.fori_loop(0, ROWS // 16, unpack, 0)

    wait_sends(faces1)
    pltpu.make_async_copy(meta_out.at[pl.ds(0, NDEV - 1)], meta_out.at[pl.ds(0, NDEV - 1)], a2a_sem.at[0]).wait()
    pltpu.make_async_copy(outgoing.at[pl.ds(0, count)], outgoing.at[pl.ds(0, count)], a2a_sem.at[2]).wait()
    pltpu.make_async_copy(replies.at[pl.ds(0, count)], replies.at[pl.ds(0, count)], a2a_sem.at[4]).wait()


def store(*refs):
    sems = refs[-1]
    pieces = CX // 2
    copies = [
        pltpu.make_async_copy(
            refs[0].at[pl.ds(2 * i, 2)], refs[4].at[pl.ds(2 * i, 2)], sems.at[i]
        )
        for i in range(pieces)
    ]
    copies += [
        pltpu.make_async_copy(refs[i], refs[4 + i], sems.at[pieces + i]) for i in range(1, 4)
    ]
    for copy in copies:
        copy.start()
    for copy in copies:
        copy.wait()


def body(temp_fluid, velocity, wall_old, wall_mask, owner_map, slot_map, temp_solid, material):
    hbm_spec = pl.BlockSpec(memory_space=pltpu.HBM)
    vmem_spec = pl.BlockSpec(memory_space=pltpu.VMEM)
    vm = pltpu.VMEM
    padded = (NT, CX + 2, CY + 2 * PADY, LN)
    dma = pltpu.SemaphoreType.DMA
    fluid, wall, solid, stress = pl.pallas_call(
        kernel,
        out_shape=(
            jax.ShapeDtypeStruct((CX, CY, NT * LN), F32),
            jax.ShapeDtypeStruct((ROWS, LN), F32),
            jax.ShapeDtypeStruct((SX, SY, LN), F32),
            jax.ShapeDtypeStruct((3, SX, SY, LN), F32),
        ),
        in_specs=[hbm_spec] * 8,
        out_specs=(vmem_spec,) * 4,
        scratch_shapes=[
            vm(padded, F32), vm(padded, F32), vm((3, CX, CY, NT * LN), BF16),
            vm((CX, CY, LN), F32), vm((CX, CY, LN), I32), vm((ROWS, LN), F32),
            vm((1, ROWS), I32), vm((1, ROWS), I32), vm((1, ROWS), I32), pltpu.SMEM((1, ROWS), I32),
            vm((NDEV * CAP, LN), F32), vm((NDEV * CAP + CAP, LN), F32),
            vm((NDEV * CAP + CAP, LN), F32), vm((NDEV * CAP, LN), F32),
            vm((NDEV, 1, LN), F32), vm((NDEV, 1, LN), F32),
            vm((SP, SR, LN), F32), vm((SP, SR, LN), F32), vm((SP, SR, LN), I32),
            vm((SP, SR, LN), F32), vm((SP, SR, LN), F32),
            vm((2, 2, NT, CX, LN), F32), vm((2, 2, NT, CX, LN), F32),
            dma((16,)), dma((3,)), dma((10,)),
            dma((2, 4)), dma((2, 4)), dma((3, 8)), dma((3, 8)),
        ],
        compiler_params=pltpu.CompilerParams(
            collective_id=0, has_side_effects=True, vmem_limit_bytes=40 * 1024 * 1024
        ),
    )(*[
        pltpu.with_memory_space_constraint(x, pltpu.HBM)
        for x in (temp_fluid, velocity, wall_old, wall_mask,
        owner_map.reshape(1, ROWS), slot_map, temp_solid, material)
    ])
    results = (fluid, wall.reshape(CX, CY, LN), solid, stress)
    return pl.pallas_call(
        store,
        out_shape=tuple(jax.ShapeDtypeStruct(r.shape, F32) for r in results),
        in_specs=[pl.BlockSpec(memory_space=pl.ANY)] * 4,
        out_specs=(pl.BlockSpec(memory_space=pl.ANY),) * 4,
        scratch_shapes=[dma((CX // 2 + 4,))],
        compiler_params=pltpu.CompilerParams(vmem_limit_bytes=1024 * 1024),
    )(*results)


def solution(mesh):
    placed = (
        P("gx", "gy", None),
        P(None, "gx", "gy", None),
        P("gx", "gy", None),
        P("gx", "gy", None),
        P(("gx", "gy"), None, None),
        P(("gx", "gy"), None),
        P("gx", "gy", None),
        P("gx", "gy", None),
    )
    return jax.shard_map(
        body,
        mesh=mesh,
        in_specs=placed,
        out_specs=(
            P("gx", "gy", None),
            P("gx", "gy", None),
            P("gx", "gy", None),
            P(None, "gx", "gy", None),
        ),
        check_vma=False,
    )
```
